32 devices in a mesh: grp: 2 (over x), bits: 16 (over z, y, core).
Axes of the slice: x: 2, y: 2, z: 4, core: 2. Of those that a mesh axis runs over, the one named last changes fastest.
Arguments:
- prefix: bfloat16 [128, 16, 1024], P(('grp', 'bits')), parts along dimension 0, may hold values from -6 to 6
- first_suffix: bfloat16 [8, 2, 512, 512], P('grp', None, 'bits'), parts along dimension 0, may hold values from -0.109375 to 0.109375
- pair_prefix: int32 [256, 3], P(('grp', 'bits')), parts along dimension 0, may hold values from 0 to 3
- pair_suffix: int32 [256, 3], P(('grp', 'bits')), parts along dimension 0, may hold values from 0 to 3, all different within a row
- merge_count: int32 [256], P(('grp', 'bits')), parts along dimension 0, may hold values from 1 to 3, as said below
- suffix: bfloat16 [32, 2, 512, 512], P(('grp', 'bits')), parts along dimension 0, may hold values from -0.1875 to 0.1875
- routes: int32 [256, 12], P(('grp', 'bits')), parts along dimension 0, may hold values from 0 to 15, all different within a row; in each aligned block of 8 rows (0 to 7, 8 to 15, ...) at most 8 rows name the same one
- cap: bfloat16 [2, 512, 64], replicated, may hold values from -0.0546875 to 0.0546875
Outputs:
- capped: float32 [256, 16, 128], P(('grp', 'bits')), parts along dimension 0
The draws below stay inside these ranges and needn't reach their ends.
There are 2 independent parts, one for each index of `grp`. The reference program is written for one: setup_inputs(seed, part) draws one part's arguments, and reference() takes and returns one part's arrays. A program takes and returns all parts, laid end to end along the dimension named above; an argument that names none is the same for every part. Nothing has to cross between parts.
Inputs may be any that keep to these rules, and one draw needn't show every extreme that they name: `pair_suffix`: each row names 3 different lifetime-one blocks. `merge_count`: some piece has exactly 3 merges and some exactly one. `routes`: each row names 12 different suffixes; in each aligned block of 8 rows no suffix is named by more than 8 rows, a bound that some block reaches.
All inputs are finite; a program needn't handle non-finite values.
Results may differ from the reference program's by a relative error of at most 0.005.
Values may be sent and summed in bfloat16 or wider, within the bound.
A program may use at most 64 MiB of HBM per device.

```python
import math
import jax
import jax.numpy as jnp
import numpy as np
from jax import lax

W = 512
CAPW = 64
PR = 16
PIECES_DEV = 8
PRE_DEV = 4
NA = 4
K1 = 3
TOP = 12
NSUF = 16
PIECES = 128
NPRE = 64
MOST = 8


def draw_merge_count(key, part):
    counts = jax.random.randint(key, (PIECES,), 1, K1 + 1)
    chosen = jax.random.randint(jax.random.fold_in(key, 7), (), 0, PIECES)
    counts = counts.at[chosen].set(K1)
    counts = counts.at[(chosen + 1) % PIECES].set(1)
    return counts.astype(jnp.int32)


def touch_ends(array, own_key, low, high):
    longest = array.shape.index(max(array.shape))
    spots = []
    for shift in (0, 1):
        where = [jax.random.randint(jax.random.fold_in(own_key, axis), (), 0, length) for axis, length in enumerate(array.shape)]
        where[longest] = (where[longest] + shift) % array.shape[longest]
        spots.append(tuple(where))
    return array.at[spots[0]].set(low).at[spots[1]].set(high)


def level_of(key, shape, cuts, least, high):
    gain = 1.0
    for axis_at, blocks in cuts:
        heights = jax.random.uniform(jax.random.fold_in(jax.random.fold_in(key, 6), axis_at), (blocks,), jnp.float32, least / len(cuts), high / len(cuts))
        gain = gain * jnp.repeat(jnp.exp(heights), shape[axis_at] // blocks).reshape((-1,) + (1,) * (len(shape) - 1 - axis_at))
    return gain


def picks_of(own_key, rows, amount, top, lift):
    order = jax.random.permutation(jax.random.fold_in(own_key, 1), amount)
    favour = order
    for power in range(3):
        favour = favour * favour // amount
    favour = favour * lift // amount
    chance = jax.random.randint(jax.random.fold_in(own_key, 2), (rows, amount), 0, 4096) + favour
    fixed_rows = jax.random.permutation(jax.random.fold_in(own_key, 3), rows)[jnp.arange(amount) % rows]
    chance = jnp.where(jnp.arange(rows)[:, None] == fixed_rows[None, :], 1 << 14, chance)
    score = chance * amount + jnp.arange(amount)
    return lax.top_k(score.astype(jnp.int32), top)[1].astype(jnp.int32)


def routed_block(key, own, number, rows, number_of, top, bound, slope):
    order = jax.random.permutation(key, number_of)
    crowded, ordinary = portions_of(number_of, rows * top, bound, slope, True), portions_of(number_of, rows * top, bound, slope, False)
    places = jnp.arange(number_of)

    def named(sizes, turn):
        used = int((sizes > 0).sum())
        fixed = max(1, used // 4)
        passed = fixed + (places - fixed + turn * (used - fixed)) % max(1, number_of - fixed)
        return jnp.zeros((number_of,), jnp.int32).at[order[jnp.where(places < fixed, places, passed)]].set(jnp.asarray(sizes, jnp.int32))

    sizes = jnp.where(number % 4 == 0, named(crowded, number // 4), named(ordinary, number - number // 4 - 1))
    mixed = jax.random.permutation(jax.random.fold_in(own, 3), number_of)
    donor, taker = mixed[0:number_of // 2 * 2:2], mixed[1:number_of // 2 * 2:2]
    margin = jnp.minimum(sizes[donor] - 1, bound - sizes[taker]) // 2
    margin = jnp.where((donor == order[0]) | (taker == order[0]) | (sizes[taker] == 0), 0, jnp.maximum(margin, 0))
    passed = jax.random.randint(jax.random.fold_in(own, 4), (number_of // 2,), 0, 1 << 20) % (margin + 1)
    sizes = sizes.at[donor].add(-passed).at[taker].add(passed)
    items = jnp.searchsorted(jnp.cumsum(sizes), jnp.arange(rows * top), side="right").astype(jnp.int32)
    listing = items.reshape(top, rows).T
    listing = listing[jax.random.permutation(jax.random.fold_in(own, 1), rows)]
    turn = jax.random.randint(jax.random.fold_in(own, 2), (rows, 1), 0, top)
    return jnp.take_along_axis(listing, (jnp.arange(top)[None, :] + turn) % top, axis=1)


def portions_of(amount, total, reach, lean, full):
    portions = [(1 << 20) // math.isqrt(rank ** lean) + 1 for rank in range(1, amount + 1)]
    largest = reach if full else min(reach, max(-(-total // amount), total * portions[0] // sum(portions)))
    least = 1 if total - largest >= amount - 1 else 0
    given, surplus = [largest] + [least] * (amount - 1), total - largest - least * (amount - 1)
    while surplus > 0:
        free = [i for i in range(1, amount) if given[i] < largest] or [i for i in range(1, amount) if given[i] < reach]
        pool, left = sum([portions[i] for i in free]), surplus
        for i in free:
            extra = min(reach - given[i], max(1, left * portions[i] // pool), surplus)
            given[i] = given[i] + extra
            surplus = surplus - extra
    return np.array(given)


def centred(stream_key, extent, spread, bound, shards=(), held_as=jnp.bfloat16):
    entries = jax.random.normal(stream_key, extent, jnp.float32) * spread
    if len(shards) > 0:
        entries = level_of(stream_key, extent, shards, -0.22, 0.18) * entries
    return jnp.clip(entries, min=-bound, max=bound).astype(held_as)


def setup_inputs(seed: int = 0, part: int = 0) -> dict:
    arg_keys = jax.random.split(jax.random.key(seed), 9)
    part_keys = jax.random.split(jax.random.fold_in(arg_keys[8], part), 9)
    prefix = centred(part_keys[0], (NPRE, PR, 2 * W), 1.0, 6.0, ((0, 16),))
    first_suffix = centred(part_keys[1], (NA, 2, W, W), (2 * W * K1) ** -0.5, 0.109375, ((2, 16),))
    pair_prefix = touch_ends(jax.random.randint(part_keys[2], (PIECES, K1), 0, PRE_DEV), jax.random.fold_in(part_keys[2], 1), 0, PRE_DEV - 1).astype(jnp.int32)
    pair_suffix = picks_of(part_keys[3], PIECES, NA, K1, 0)
    merge_count = draw_merge_count(jax.random.fold_in(jax.random.fold_in(arg_keys[8], part), 71), part)
    suffix = centred(part_keys[5], (NSUF, 2, W, W), (2 * W) ** -0.5, 0.1875, ((0, 16),))
    routes_keys = jax.random.split(jax.random.fold_in(part_keys[6], 1), PIECES // PIECES_DEV)
    routes_turns = jax.random.permutation(jax.random.fold_in(part_keys[6], 3), PIECES // PIECES_DEV)
    routes = jax.vmap(lambda own, number: routed_block(jax.random.fold_in(part_keys[6], 2), own, number, PIECES_DEV, NSUF, TOP, MOST, 2))(routes_keys, routes_turns).reshape((PIECES, TOP))
    cap = centred(arg_keys[7], (2, W, CAPW), (2 * W * TOP) ** -0.5, 0.0546875)
    return dict(prefix=prefix, first_suffix=first_suffix, pair_prefix=pair_prefix, pair_suffix=pair_suffix, merge_count=merge_count, suffix=suffix, routes=routes, cap=cap)


HIGHEST_PRECISION = lax.Precision.HIGHEST


def complex_form(blocks):
    real_part = blocks[..., 0, :, :]
    imag_part = blocks[..., 1, :, :]
    upper_half = jnp.concatenate([real_part, imag_part], axis=-1)
    lower_half = jnp.concatenate([-imag_part, real_part], axis=-1)
    return jnp.concatenate([upper_half, lower_half], axis=-2)


def reference(prefix, first_suffix, pair_prefix, pair_suffix, merge_count, suffix, routes, cap):
    first_forms = complex_form(first_suffix.astype(jnp.float32))
    cap_form = complex_form(cap.astype(jnp.float32))

    def one_piece(piece_index):
        owner_index = piece_index // PIECES_DEV
        prefix_rows = prefix[PRE_DEV * owner_index + pair_prefix[piece_index]].astype(jnp.float32)
        block_forms = first_forms[pair_suffix[piece_index]]
        live_mask = (jnp.arange(K1, dtype=jnp.int32) < merge_count[piece_index]).astype(jnp.float32)
        merge_terms = jnp.einsum("krc,kcw->krw", prefix_rows, block_forms, precision=HIGHEST_PRECISION)
        state_rows = jnp.sum(merge_terms * live_mask[:, None, None], axis=0).astype(jnp.bfloat16)
        state_rows = lax.optimization_barrier(state_rows).astype(jnp.float32)
        chosen = complex_form(suffix[routes[piece_index]].astype(jnp.float32))
        partial_value = jnp.einsum("rc,kcw->krw", state_rows, chosen, precision=HIGHEST_PRECISION).astype(jnp.bfloat16)
        partial_value = lax.optimization_barrier(partial_value).astype(jnp.float32)
        merged = jnp.sum(partial_value, axis=0)
        return jnp.dot(merged, cap_form, precision=HIGHEST_PRECISION)

    return lax.map(one_piece, jnp.arange(PIECES, dtype=jnp.int32))
```

```python
import jax
import jax.numpy as jnp
from jax import lax
from jax.experimental import pallas as pl
from jax.experimental.pallas import tpu as pltpu
from jax.sharding import PartitionSpec as P

HIGHEST_PRECISION = lax.Precision.HIGHEST


def complex_form(blocks):
    real_part = blocks[..., 0, :, :]
    imag_part = blocks[..., 1, :, :]
    upper_half = jnp.concatenate([real_part, imag_part], axis=-1)
    lower_half = jnp.concatenate([-imag_part, real_part], axis=-1)
    return jnp.concatenate([upper_half, lower_half], axis=-2)


def on_device_sparse(prefix, first_suffix, pair_prefix, pair_suffix, merge_count, suffix, routes, cap):
    pieces = pair_prefix.shape[0]
    merges = pair_prefix.shape[1]
    held_blocks = prefix.shape[0]
    rows_piece = prefix.shape[1]
    twice_width = prefix.shape[2]
    half_width = twice_width // 2
    first_count = first_suffix.shape[0]
    listed = routes.shape[1]
    owners = lax.axis_size("bits")
    slot_count = min(pieces, max(2, (2 * pieces * listed + owners - 1) // owners))
    live_mask = lax.broadcasted_iota(jnp.int32, (pieces, merges), 1) < merge_count[:, None]
    matches = (
        pair_suffix[:, :, None] == lax.broadcasted_iota(jnp.int32, (pieces, merges, first_count), 2)
    ) & live_mask[:, :, None]
    which_block = pair_prefix[:, :, None] == lax.broadcasted_iota(
        jnp.int32, (pieces, merges, held_blocks), 2
    )
    prefix_picks = jnp.einsum(
        "ika,ikp->iap", matches.astype(jnp.float32), which_block.astype(jnp.float32)
    ).astype(jnp.bfloat16)
    selected = jnp.einsum(
        "iap,prc->airc", prefix_picks, prefix, preferred_element_type=jnp.float32
    ).astype(jnp.bfloat16)
    selected = selected.reshape(first_count, pieces * rows_piece, twice_width)
    portion = lax.all_gather(first_suffix, "bits", axis=2, tiled=True)
    count_rows = portion.shape[2]
    real_cols = lax.slice_in_dim(selected, 0, count_rows, axis=2)
    imag_cols = lax.dynamic_slice_in_dim(selected, half_width, count_rows, 2)
    left_side = jnp.concatenate([real_cols, imag_cols], axis=2)
    upper_half = jnp.concatenate([portion[:, 0], portion[:, 1]], axis=2)
    lower_half = jnp.concatenate([-portion[:, 1], portion[:, 0]], axis=2)
    right_side = jnp.concatenate([upper_half, lower_half], axis=1)
    state_rows = jnp.einsum(
        "arc,acw->rw", left_side, right_side, preferred_element_type=jnp.float32
    )
    state_rows = state_rows.astype(jnp.bfloat16).reshape(pieces, rows_piece, twice_width)
    named_by = jnp.sum(
        (routes[:, :, None] == lax.broadcasted_iota(jnp.int32, (pieces, listed, owners), 2)).astype(
            jnp.int32
        ),
        axis=1,
    )
    earlier = lax.broadcasted_iota(jnp.int32, (pieces, pieces), 0) > lax.broadcasted_iota(
        jnp.int32, (pieces, pieces), 1
    )
    slot_rank = jnp.einsum(
        "ij,jd->id", earlier.astype(jnp.float32), named_by.astype(jnp.float32),
        precision=HIGHEST_PRECISION,
    ).astype(jnp.int32)
    slot_hit = (
        slot_rank[:, :, None] == lax.broadcasted_iota(jnp.int32, (pieces, owners, slot_count), 2)
    ) & (named_by[:, :, None] > 0)
    dispatch = jnp.transpose(slot_hit, (1, 2, 0)).astype(jnp.bfloat16)
    outgoing = jnp.einsum(
        "dmi,irc->dmrc", dispatch, state_rows, preferred_element_type=jnp.float32
    ).astype(jnp.bfloat16)
    own_form = complex_form(suffix[0])
    cap_form = complex_form(cap)
    products = jnp.einsum(
        "smrc,cw->smrw",
        lax.all_to_all(outgoing, "bits", split_axis=0, concat_axis=0, tiled=True),
        own_form,
        preferred_element_type=jnp.float32,
    ).astype(jnp.bfloat16)
    capped_terms = jnp.einsum(
        "smrw,wv->smrv", products, cap_form, preferred_element_type=jnp.float32
    )
    returned = lax.all_to_all(
        capped_terms.astype(jnp.bfloat16), "bits", split_axis=0, concat_axis=0, tiled=True
    ).astype(capped_terms.dtype)
    return jnp.einsum(
        "dmi,dmrv->irv", dispatch.astype(jnp.float32), returned, precision=HIGHEST_PRECISION
    )


def weights_of(pair_prefix, pair_suffix, merge_count, held_blocks, first_count):
    pieces, merges = pair_prefix.shape
    live_mask = lax.broadcasted_iota(jnp.int32, (pieces, merges), 1) < merge_count[:, None]
    matches = (
        pair_suffix[:, :, None] == lax.broadcasted_iota(jnp.int32, (pieces, merges, first_count), 2)
    ) & live_mask[:, :, None]
    which_block = pair_prefix[:, :, None] == lax.broadcasted_iota(
        jnp.int32, (pieces, merges, held_blocks), 2
    )
    return jnp.sum(
        (matches[:, :, :, None] & which_block[:, :, None, :]).astype(jnp.float32), axis=1
    ).astype(jnp.bfloat16)


def on_device_dense(prefix, first_suffix, pair_prefix, pair_suffix, merge_count, suffix, routes, cap):
    pieces = pair_prefix.shape[0]
    held_blocks, rows_piece, twice_width = prefix.shape
    first_count = first_suffix.shape[0]
    owners = lax.axis_size("bits")
    listed = routes.shape[1]
    portion = lax.all_gather(first_suffix, "bits", axis=2, tiled=True)
    cap_form = jnp.concatenate([cap[0], cap[1]], axis=1)
    cap_turn = jnp.concatenate([-cap[1], cap[0]], axis=1)
    closed = (
        jnp.dot(suffix[0, 0], cap_form, preferred_element_type=jnp.float32)
        + jnp.dot(suffix[0, 1], cap_turn, preferred_element_type=jnp.float32)
    ).astype(jnp.bfloat16)
    closed_all = lax.all_gather(closed, "bits", axis=1, tiled=False)
    picks = weights_of(pair_prefix, pair_suffix, merge_count, held_blocks, first_count)
    selected = jnp.einsum(
        "iap,prc->airc", picks, prefix, preferred_element_type=jnp.float32
    ).astype(jnp.bfloat16)
    selected = selected.reshape(first_count, pieces * rows_piece, twice_width)
    half = twice_width // 2
    real = selected[:, :, :half]
    imag = selected[:, :, half:]
    by_real = jnp.einsum(
        "arc,acw->rw", jnp.concatenate([real, -imag], axis=2),
        portion.reshape(first_count, twice_width, half), preferred_element_type=jnp.float32,
    )
    by_imag = jnp.einsum(
        "arc,acw->rw", jnp.concatenate([imag, real], axis=2),
        portion.reshape(first_count, twice_width, half), preferred_element_type=jnp.float32,
    )
    state_real = by_real.astype(jnp.bfloat16)
    state_imag = by_imag.astype(jnp.bfloat16)
    flat = closed_all.reshape(half, -1)
    capw = cap.shape[2]
    stacked = jnp.concatenate([state_real, state_imag], axis=0)
    both = jnp.dot(stacked, flat, preferred_element_type=jnp.float32)
    both = both.reshape(2, pieces, rows_piece, owners, 2, capw)
    named = jnp.sum(
        (routes[:, :, None] == lax.broadcasted_iota(jnp.int32, (pieces, listed, owners), 2)).astype(
            jnp.float32
        ),
        axis=1,
    )
    summed = jnp.sum(both * named[None, :, None, :, None, None], axis=3)
    out_real = summed[0, :, :, 0] - summed[1, :, :, 1]
    out_imag = summed[0, :, :, 1] + summed[1, :, :, 0]
    return jnp.concatenate([out_real, out_imag], axis=-1)


BF = jnp.bfloat16
F32 = jnp.float32


def flip(value, pattern):
    bit = 1
    while bit <= pattern:
        if pattern & bit:
            value = value + bit - 2 * bit * ((value // bit) % 2)
        bit *= 2
    return value


def iota(shape, axis):
    return lax.broadcasted_iota(jnp.int32, shape, axis)


PLANES = 4


def both_parts(real, imag, lanes):
    count = real.shape[0] // 16
    stacked = jnp.stack(
        [real.reshape(count, 16, lanes), imag.reshape(count, 16, lanes)], axis=1
    )
    return stacked.reshape(2 * real.shape[0], lanes)


def planes_kernel(
    sizes, x_ref, pp_ref, ps_ref, count_ref, route_ref, f_hbm, s_hbm, cap_ref, out_ref,
    s_ref, qsend, qall, fall, mt, mall, sel, xy, expand, masks, gall, acc, place, ret_out, ret_in,
    local, q_send, q_recv, q_bulk, f_send, f_recv, m_send, m_recv, r_send, r_recv,
):
    first_count, held, rows_piece, pieces, depth, half, wide = sizes
    rows = pieces * rows_piece
    held_rows = held * rows_piece
    span = half // PLANES
    base = first_count * held
    two = 2 * wide
    me = lax.axis_index("bits")
    z = me // 4
    j = me % 4
    y = j // 2
    middle = (z == 1) | (z == 2)

    def near(pattern):
        return flip(z, pattern)

    def beside(pattern):
        return flip(j, pattern)

    def send(src, dst, send_sem, recv_sem, plane, seat):
        return pltpu.make_async_remote_copy(
            src_ref=src, dst_ref=dst, send_sem=send_sem, recv_sem=recv_sem,
            device_id={"bits": 4 * plane + seat}, device_id_type=pl.DeviceIdType.MESH,
        )

    barrier = pltpu.get_barrier_semaphore()
    for p in range(PLANES):
        for s in range(4):
            if p or s:
                pl.semaphore_signal(
                    barrier, inc=1, device_id={"bits": 4 * near(p) + beside(s)},
                    device_id_type=pl.DeviceIdType.MESH,
                )
    s_copy = pltpu.make_async_copy(s_hbm, s_ref, local.at[0])
    s_copy.start()
    f_local = pltpu.make_async_copy(f_hbm, fall.at[:, :, j], local.at[1])
    f_local.start()

    eye = iota((pieces, pieces), 0) == iota((pieces, pieces), 1)

    def column(row):
        spread = jnp.broadcast_to(row, (pieces, pieces))
        return jnp.sum(jnp.where(eye, spread, 0), axis=1, keepdims=True)

    spot = iota((pieces, wide), 1)
    count = column(count_ref[...])
    table = jnp.zeros((pieces, wide), F32)
    for k in range(pp_ref.shape[0]):
        code = column(ps_ref[k:k + 1, :]) * held + column(pp_ref[k:k + 1, :])
        table = table + jnp.where((spot == code) & (count > k), 1.0, 0.0)
    for k in range(route_ref.shape[1]):
        table = table + jnp.where(spot == route_ref[:, k:k + 1] + base, 1.0, 0.0)
    table = jnp.concatenate([table, jnp.zeros((16 - pieces, wide), F32)], axis=0).astype(BF)
    for p in range(PLANES):
        qsend[p, :held_rows, :wide] = x_ref[:, p * span:(p + 1) * span]
        qsend[p, :held_rows, wide:] = x_ref[:, half + p * span:half + (p + 1) * span]
        qsend[p, held_rows:, :wide] = table
        qsend[p, held_rows:, wide:] = jnp.zeros((16, wide), BF)
    qall[j, z] = qsend[z]

    line = iota((wide, two), 0)
    xy[:, :two] = jnp.where(iota((wide, two), 1) // rows_piece == line, 1.0, 0.0).astype(BF)
    reach = PLANES * wide
    line = iota((wide, reach), 0)
    xy[:, two:] = jnp.where(iota((wide, reach), 1) // 32 + base == line, 1.0, 0.0).astype(BF)
    for q in range(4):
        lane = iota((wide, reach), 0)
        col = iota((wide, reach), 1)
        inside = lane % 32
        goal = (lane // 32) * wide + (inside // 16) * (wide // 2) + 16 * q + inside % 16
        place[q * wide:(q + 1) * wide, :] = jnp.where(col == goal, 1.0, 0.0).astype(BF)

    s_copy.wait()

    def times(left, part):
        return lax.dot_general(
            left, s_ref[part], (((1,), (1,)), ((), ())), preferred_element_type=F32
        )

    upper = both_parts(cap_ref[0], cap_ref[1], half)
    lower = both_parts(-cap_ref[1], cap_ref[0], half)
    closed = (times(upper, 0) + times(lower, 1)).astype(BF)
    mt[...] = closed.reshape(4, 32, half)
    mall[z, j] = mt[j]

    def m_near(t, s):
        return send(
            mt.at[beside(s)], mall.at[z, j], m_send.at[0, t, s], m_recv.at[z, y], near(t),
            beside(s),
        )

    def m_quad(s):
        side = flip(y, 1) if False else y
        return send(
            mt.at[beside(s)], mall.at[z, j], m_send.at[0, 0, s], m_recv.at[z, side], z, beside(s)
        )

    def m_pair(source, side, t, index):
        block = mall.at[source, pl.ds(2 * side, 2)]
        return send(
            block, block, m_send.at[1, t, index], m_recv.at[source, side], near(t), j
        )

    def m_arrived(source, side):
        block = mall.at[source, pl.ds(2 * side, 2)]
        send(block, block, m_send.at[0, 0, 0], m_recv.at[source, side], z, beside(1)).wait_recv()

    def q_line(t):
        return send(
            qsend.at[near(t)], qall.at[j, z], q_send.at[0, t], q_recv.at[j, z], near(t), j
        )

    def q_across(p):
        return send(
            qall.at[j, p], qall.at[j, p], q_send.at[1, p], q_recv.at[j, p], z, beside(2)
        )

    def q_core(s, index):
        return send(
            qall.at[beside(s)], qall.at[beside(s)], q_send.at[2, index], q_bulk.at[beside(s)], z,
            beside(1),
        )

    def q_arrived(seat, plane):
        block = qall.at[seat, plane]
        send(block, block, q_send.at[0, 0], q_recv.at[seat, plane], z, beside(1)).wait_recv()

    def q_bulk_arrived(seat):
        block = qall.at[seat]
        send(block, block, q_send.at[0, 0], q_bulk.at[seat], z, beside(1)).wait_recv()

    def f_copy(s):
        return send(f_hbm, fall.at[:, :, j], f_send.at[s], f_recv.at[j], z, beside(s))

    def f_pass():
        seat = beside(2)
        block = fall.at[:, :, seat]
        return send(block, block, f_send.at[0], f_recv.at[seat], z, beside(1))

    def f_arrived(seat):
        block = fall.at[:, :, seat]
        send(block, block, f_send.at[0], f_recv.at[seat], z, beside(1)).wait_recv()

    same = jnp.where(
        iota((rows_piece, two), 0) == iota((rows_piece, two), 1) % rows_piece, 1.0, 0.0
    ).astype(F32)

    def prepare(seat):
        tabs = jnp.concatenate(
            [qall[seat, p, held_rows:, :wide] for p in range(PLANES)], axis=0
        )
        spread = jnp.dot(tabs, xy[...], preferred_element_type=F32)
        expand[...] = spread[:, :two].reshape(PLANES, 16, two)
        for p in range(PLANES):
            part = spread[:, two + p * wide:two + (p + 1) * wide]
            masks[p, seat] = part.reshape(PLANES, 16, wide)[:, :pieces]

        def one(p, carry):
            wanted = expand[p][:pieces]
            kept = jnp.broadcast_to(wanted[:, None, :], (pieces, rows_piece, two)) * same[None]
            kept = kept.reshape(rows, two)
            group = iota((rows, two), 1) // held_rows
            left = jnp.concatenate(
                [jnp.where(group == a, kept, 0.0).astype(BF) for a in range(first_count)], axis=0
            )
            right = jnp.concatenate([qall[seat, p, :held_rows]] * first_count, axis=0)
            picked = jnp.dot(left, right, preferred_element_type=F32).astype(BF)
            for a in range(first_count):
                sel[seat, p, :, a * two:(a + 1) * two] = picked[a * rows:(a + 1) * rows]
            return carry

        lax.fori_loop(0, PLANES, one, 0)

    def gather(b, planes):
        left = jnp.concatenate([mall[p].reshape(wide, half) for p in planes], axis=0)
        for a in range(first_count):
            product = lax.dot_general(
                left, fall[a].reshape(two, half), (((1,), (1,)), ((), ())),
                preferred_element_type=F32,
            ).reshape(len(planes) * 4, 2, 16, two)
            real = product[:, 0, :, :wide] - product[:, 1, :, wide:]
            imag = product[:, 0, :, wide:] + product[:, 1, :, :wide]
            joined = jnp.stack(
                [jnp.concatenate([real, -imag], axis=-1), jnp.concatenate([imag, real], axis=-1)],
                axis=1,
            )
            gall[b, :, a * two:(a + 1) * two] = joined.reshape(len(planes) * wide, two).astype(BF)

    def part(b, planes, seat):
        lines = sel[seat].reshape(PLANES * rows, first_count * two)
        values = lax.dot_general(
            lines, gall[b], (((1,), (1,)), ((), ())), preferred_element_type=F32
        )
        total = None
        for u, p in enumerate(planes):
            mask = masks[p, seat].reshape(PLANES * pieces, 1, wide)
            mask = jnp.broadcast_to(mask, (PLANES * pieces, rows_piece, wide))
            term = values[:, u * wide:(u + 1) * wide] * mask.reshape(PLANES * rows, wide)
            total = term if total is None else total + term
        return total

    pl.semaphore_wait(barrier, 4 * PLANES - 1)
    for s in (2, 3, 1):
        m_quad(s).start()
    for s in (0, 1):
        for t in (2, 1):
            m_near(t, s).start()

    @pl.when(middle)
    def _():
        for s in (0, 1):
            m_near(3, s).start()

    for t in (3, 2, 1):
        q_line(t).start()
    q_across(z).start()
    for s in (2, 1):
        f_copy(s).start()

    m_arrived(z, flip(y, 1))
    for t in (2, 1):
        m_pair(z, flip(y, 1), t, 0).start()

    @pl.when(middle)
    def _():
        m_pair(z, flip(y, 1), 3, 0).start()

    for t in (1, 2, 3):
        q_arrived(j, near(t))
        q_across(near(t)).start()
    q_core(0, 0).start()

    @pl.when(middle)
    def _():
        m_arrived(near(2), y)
        m_pair(near(2), y, 1, 1).start()

    prepare(j)
    for t in (0, 1, 2, 3):
        q_arrived(beside(2), near(t))
    q_core(2, 1).start()

    @pl.when(middle)
    def _():
        m_arrived(near(2), flip(y, 1))
        m_pair(near(2), flip(y, 1), 1, 2).start()

    prepare(beside(2))
    f_arrived(beside(2))
    f_pass().start()
    for s in (1, 3):
        q_bulk_arrived(beside(s))
        prepare(beside(s))
    send(
        mt.at[j], mall.at[z, beside(1)], m_send.at[0, 0, 0], m_recv.at[z, y], z, beside(1)
    ).wait_recv()
    f_local.wait()
    f_arrived(beside(1))
    f_arrived(beside(3))
    m_arrived(near(1), y)
    m_arrived(near(1), flip(y, 1))
    early = (z, near(1))
    gather(0, early)

    def first_half(seat, carry):
        acc[seat] = part(0, early, seat)
        return carry

    lax.fori_loop(0, 4, first_half, 0)

    @pl.when(jnp.logical_not(middle))
    def _():
        m_arrived(near(2), y)
        m_arrived(near(2), flip(y, 1))

    m_arrived(near(3), y)
    m_arrived(near(3), flip(y, 1))
    late = (near(2), near(3))
    gather(1, late)

    def ret_copy(t, s):
        return send(
            ret_out.at[beside(s), near(t)], ret_in.at[j, z], r_send.at[s, t], r_recv.at[j, z],
            near(t), beside(s),
        )

    group = iota((32, wide), 1) // 32
    for s in (3, 2, 1, 0):
        seat = beside(s)
        total = acc[seat] + part(1, late, seat)
        total = total + pltpu.roll(total, wide // 2, 1)
        total = total + pltpu.roll(total, wide // 4, 1)
        total = total.reshape(PLANES, 4, 32, wide)
        packed = total[:, 3]
        for b in (2, 1, 0):
            packed = jnp.where(group == b, total[:, b], packed)
        ret_out[seat] = packed.astype(BF)
        for t in (3, 2, 1, 0):
            if s or t:
                ret_copy(t, s).start()
    ret_in[j, z] = ret_out[j, z]
    for s in (0, 1, 2, 3):
        for t in range(PLANES):
            if s or t:
                block = ret_in.at[beside(s), near(t)]
                send(
                    block, block, r_send.at[0, 0], r_recv.at[beside(s), near(t)], z, beside(1)
                ).wait_recv()
    left = jnp.concatenate([ret_in[q].reshape(wide, wide) for q in range(4)], axis=1)
    placed = jnp.dot(left, place[...], preferred_element_type=F32).reshape(PLANES, 32, reach)
    summed = jnp.sum(placed, axis=0)
    for b in range(4):
        out_ref[b * 32:(b + 1) * 32] = summed[:, b * wide:(b + 1) * wide]

    for s in (2, 3, 1):
        m_quad(s).wait_send()
    for s in (0, 1):
        for t in (2, 1):
            m_near(t, s).wait_send()
    for t in (2, 1):
        m_pair(z, flip(y, 1), t, 0).wait_send()

    @pl.when(middle)
    def _():
        for s in (0, 1):
            m_near(3, s).wait_send()
        m_pair(z, flip(y, 1), 3, 0).wait_send()
        m_pair(near(2), y, 1, 1).wait_send()
        m_pair(near(2), flip(y, 1), 1, 2).wait_send()

    for t in (3, 2, 1):
        q_line(t).wait_send()
    for p in range(PLANES):
        q_across(near(p)).wait_send()
    q_core(0, 0).wait_send()
    q_core(2, 1).wait_send()
    for s in (2, 1):
        f_copy(s).wait_send()
    f_pass().wait_send()
    for s in range(4):
        for t in range(PLANES):
            if s or t:
                ret_copy(t, s).wait_send()


def on_device_planes(prefix, first_suffix, pair_prefix, pair_suffix, merge_count, suffix, routes, cap):
    pieces = pair_prefix.shape[0]
    held, rows_piece, twice_width = prefix.shape
    half = twice_width // 2
    first_count, _, depth, _ = first_suffix.shape
    wide = 2 * cap.shape[2]
    rows = pieces * rows_piece
    held_rows = held * rows_piece
    two = 2 * wide
    sizes = (first_count, held, rows_piece, pieces, depth, half, wide)
    vmem = pl.BlockSpec(memory_space=pltpu.VMEM)
    hbm = pl.BlockSpec(memory_space=pl.ANY)
    dma = pltpu.SemaphoreType.DMA
    out = pl.pallas_call(
        lambda *refs: planes_kernel(sizes, *refs),
        name="planes",
        out_shape=jax.ShapeDtypeStruct((rows, wide), F32),
        in_specs=[vmem, vmem, vmem, vmem, vmem, hbm, hbm, vmem],
        out_specs=vmem,
        scratch_shapes=[
            pltpu.VMEM((2, half, half), BF),
            pltpu.VMEM((PLANES, held_rows + 16, two), BF),
            pltpu.VMEM((4, PLANES, held_rows + 16, two), BF),
            pltpu.VMEM((first_count, 2, 4, depth, half), BF),
            pltpu.VMEM((4, 32, half), BF),
            pltpu.VMEM((PLANES, 4, 32, half), BF),
            pltpu.VMEM((4, PLANES, rows, first_count * two), BF),
            pltpu.VMEM((wide, two + PLANES * wide), BF),
            pltpu.VMEM((PLANES, 16, two), F32),
            pltpu.VMEM((PLANES, 4, PLANES, pieces, wide), F32),
            pltpu.VMEM((2, two, first_count * two), BF),
            pltpu.VMEM((4, PLANES * rows, wide), F32),
            pltpu.VMEM((4 * wide, PLANES * wide), BF),
            pltpu.VMEM((4, PLANES, 32, wide), BF),
            pltpu.VMEM((4, PLANES, 32, wide), BF),
            dma((2,)), dma((3, 4)), dma((4, PLANES)), dma((4,)), dma((3,)), dma((4,)),
            dma((2, PLANES, 4)), dma((PLANES, 2)), dma((4, PLANES)), dma((4, PLANES)),
        ],
        compiler_params=pltpu.CompilerParams(
            collective_id=0, has_side_effects=True, vmem_limit_bytes=40 * 2 ** 20
        ),
    )(
        prefix.reshape(held_rows, twice_width), pair_prefix.T, pair_suffix.T, merge_count[None],
        routes, first_suffix, suffix[0], cap.transpose(0, 2, 1),
    )
    return out.reshape(pieces, rows_piece, wide)


def on_device(prefix, first_suffix, pair_prefix, pair_suffix, merge_count, suffix, routes, cap):
    pieces = pair_prefix.shape[0]
    listed = routes.shape[1]
    owners = lax.axis_size("bits")
    slots = min(pieces, max(2, (2 * pieces * listed + owners - 1) // owners))
    held, rows_piece, twice_width = prefix.shape
    wide = 2 * cap.shape[2]
    fits = (
        owners == 4 * PLANES and wide == 128 and pieces == 8 and rows_piece == 16
        and twice_width == 2 * PLANES * wide and first_suffix.shape[0] * held == rows_piece
        and held * rows_piece * first_suffix.shape[0] == 2 * wide and suffix.shape[0] == 1
        and owners * first_suffix.shape[2] == twice_width // 2 and owners <= wide - rows_piece
    )
    body = on_device_sparse
    if slots == pieces:
        body = on_device_planes if fits else on_device_dense
    return body(
        prefix, first_suffix, pair_prefix, pair_suffix, merge_count, suffix, routes, cap
    )


def solution(mesh):
    return jax.shard_map(
        on_device,
        mesh=mesh,
        in_specs=(
            P(("grp", "bits"), None, None),
            P("grp", None, "bits", None),
            P(("grp", "bits"), None),
            P(("grp", "bits"), None),
            P(("grp", "bits")),
            P(("grp", "bits"), None, None, None),
            P(("grp", "bits"), None),
            P(),
        ),
        out_specs=P(("grp", "bits"), None, None),
        check_vma=False,
    )
```

```python
import jax
import jax.numpy as jnp
from jax import lax
from jax.experimental import pallas as pl
from jax.experimental.pallas import tpu as pltpu
from jax.sharding import PartitionSpec as P

HIGHEST_PRECISION = lax.Precision.HIGHEST


def complex_form(blocks):
    real_part = blocks[..., 0, :, :]
    imag_part = blocks[..., 1, :, :]
    upper_half = jnp.concatenate([real_part, imag_part], axis=-1)
    lower_half = jnp.concatenate([-imag_part, real_part], axis=-1)
    return jnp.concatenate([upper_half, lower_half], axis=-2)


def on_device_sparse(prefix, first_suffix, pair_prefix, pair_suffix, merge_count, suffix, routes, cap):
    pieces = pair_prefix.shape[0]
    merges = pair_prefix.shape[1]
    held_blocks = prefix.shape[0]
    rows_piece = prefix.shape[1]
    twice_width = prefix.shape[2]
    half_width = twice_width // 2
    first_count = first_suffix.shape[0]
    listed = routes.shape[1]
    owners = lax.axis_size("bits")
    slot_count = min(pieces, max(2, (2 * pieces * listed + owners - 1) // owners))
    live_mask = lax.broadcasted_iota(jnp.int32, (pieces, merges), 1) < merge_count[:, None]
    matches = (
        pair_suffix[:, :, None] == lax.broadcasted_iota(jnp.int32, (pieces, merges, first_count), 2)
    ) & live_mask[:, :, None]
    which_block = pair_prefix[:, :, None] == lax.broadcasted_iota(
        jnp.int32, (pieces, merges, held_blocks), 2
    )
    prefix_picks = jnp.einsum(
        "ika,ikp->iap", matches.astype(jnp.float32), which_block.astype(jnp.float32)
    ).astype(jnp.bfloat16)
    selected = jnp.einsum(
        "iap,prc->airc", prefix_picks, prefix, preferred_element_type=jnp.float32
    ).astype(jnp.bfloat16)
    selected = selected.reshape(first_count, pieces * rows_piece, twice_width)
    portion = lax.all_gather(first_suffix, "bits", axis=2, tiled=True)
    count_rows = portion.shape[2]
    real_cols = lax.slice_in_dim(selected, 0, count_rows, axis=2)
    imag_cols = lax.dynamic_slice_in_dim(selected, half_width, count_rows, 2)
    left_side = jnp.concatenate([real_cols, imag_cols], axis=2)
    upper_half = jnp.concatenate([portion[:, 0], portion[:, 1]], axis=2)
    lower_half = jnp.concatenate([-portion[:, 1], portion[:, 0]], axis=2)
    right_side = jnp.concatenate([upper_half, lower_half], axis=1)
    state_rows = jnp.einsum(
        "arc,acw->rw", left_side, right_side, preferred_element_type=jnp.float32
    )
    state_rows = state_rows.astype(jnp.bfloat16).reshape(pieces, rows_piece, twice_width)
    named_by = jnp.sum(
        (routes[:, :, None] == lax.broadcasted_iota(jnp.int32, (pieces, listed, owners), 2)).astype(
            jnp.int32
        ),
        axis=1,
    )
    earlier = lax.broadcasted_iota(jnp.int32, (pieces, pieces), 0) > lax.broadcasted_iota(
        jnp.int32, (pieces, pieces), 1
    )
    slot_rank = jnp.einsum(
        "ij,jd->id", earlier.astype(jnp.float32), named_by.astype(jnp.float32),
        precision=HIGHEST_PRECISION,
    ).astype(jnp.int32)
    slot_hit = (
        slot_rank[:, :, None] == lax.broadcasted_iota(jnp.int32, (pieces, owners, slot_count), 2)
    ) & (named_by[:, :, None] > 0)
    dispatch = jnp.transpose(slot_hit, (1, 2, 0)).astype(jnp.bfloat16)
    outgoing = jnp.einsum(
        "dmi,irc->dmrc", dispatch, state_rows, preferred_element_type=jnp.float32
    ).astype(jnp.bfloat16)
    own_form = complex_form(suffix[0])
    cap_form = complex_form(cap)
    products = jnp.einsum(
        "smrc,cw->smrw",
        lax.all_to_all(outgoing, "bits", split_axis=0, concat_axis=0, tiled=True),
        own_form,
        preferred_element_type=jnp.float32,
    ).astype(jnp.bfloat16)
    capped_terms = jnp.einsum(
        "smrw,wv->smrv", products, cap_form, preferred_element_type=jnp.float32
    )
    returned = lax.all_to_all(
        capped_terms.astype(jnp.bfloat16), "bits", split_axis=0, concat_axis=0, tiled=True
    ).astype(capped_terms.dtype)
    return jnp.einsum(
        "dmi,dmrv->irv", dispatch.astype(jnp.float32), returned, precision=HIGHEST_PRECISION
    )


def weights_of(pair_prefix, pair_suffix, merge_count, held_blocks, first_count):
    pieces, merges = pair_prefix.shape
    live_mask = lax.broadcasted_iota(jnp.int32, (pieces, merges), 1) < merge_count[:, None]
    matches = (
        pair_suffix[:, :, None] == lax.broadcasted_iota(jnp.int32, (pieces, merges, first_count), 2)
    ) & live_mask[:, :, None]
    which_block = pair_prefix[:, :, None] == lax.broadcasted_iota(
        jnp.int32, (pieces, merges, held_blocks), 2
    )
    return jnp.sum(
        (matches[:, :, :, None] & which_block[:, :, None, :]).astype(jnp.float32), axis=1
    ).astype(jnp.bfloat16)


def on_device_dense(prefix, first_suffix, pair_prefix, pair_suffix, merge_count, suffix, routes, cap):
    pieces = pair_prefix.shape[0]
    held_blocks, rows_piece, twice_width = prefix.shape
    first_count = first_suffix.shape[0]
    owners = lax.axis_size("bits")
    listed = routes.shape[1]
    portion = lax.all_gather(first_suffix, "bits", axis=2, tiled=True)
    cap_form = jnp.concatenate([cap[0], cap[1]], axis=1)
    cap_turn = jnp.concatenate([-cap[1], cap[0]], axis=1)
    closed = (
        jnp.dot(suffix[0, 0], cap_form, preferred_element_type=jnp.float32)
        + jnp.dot(suffix[0, 1], cap_turn, preferred_element_type=jnp.float32)
    ).astype(jnp.bfloat16)
    closed_all = lax.all_gather(closed, "bits", axis=1, tiled=False)
    picks = weights_of(pair_prefix, pair_suffix, merge_count, held_blocks, first_count)
    selected = jnp.einsum(
        "iap,prc->airc", picks, prefix, preferred_element_type=jnp.float32
    ).astype(jnp.bfloat16)
    selected = selected.reshape(first_count, pieces * rows_piece, twice_width)
    half = twice_width // 2
    real = selected[:, :, :half]
    imag = selected[:, :, half:]
    by_real = jnp.einsum(
        "arc,acw->rw", jnp.concatenate([real, -imag], axis=2),
        portion.reshape(first_count, twice_width, half), preferred_element_type=jnp.float32,
    )
    by_imag = jnp.einsum(
        "arc,acw->rw", jnp.concatenate([imag, real], axis=2),
        portion.reshape(first_count, twice_width, half), preferred_element_type=jnp.float32,
    )
    state_real = by_real.astype(jnp.bfloat16)
    state_imag = by_imag.astype(jnp.bfloat16)
    flat = closed_all.reshape(half, -1)
    capw = cap.shape[2]
    stacked = jnp.concatenate([state_real, state_imag], axis=0)
    both = jnp.dot(stacked, flat, preferred_element_type=jnp.float32)
    both = both.reshape(2, pieces, rows_piece, owners, 2, capw)
    named = jnp.sum(
        (routes[:, :, None] == lax.broadcasted_iota(jnp.int32, (pieces, listed, owners), 2)).astype(
            jnp.float32
        ),
        axis=1,
    )
    summed = jnp.sum(both * named[None, :, None, :, None, None], axis=3)
    out_real = summed[0, :, :, 0] - summed[1, :, :, 1]
    out_imag = summed[0, :, :, 1] + summed[1, :, :, 0]
    return jnp.concatenate([out_real, out_imag], axis=-1)


BF = jnp.bfloat16
F32 = jnp.float32


def flip(value, pattern):
    bit = 1
    while bit <= pattern:
        if pattern & bit:
            value = value + bit - 2 * bit * ((value // bit) % 2)
        bit *= 2
    return value


def iota(shape, axis):
    return lax.broadcasted_iota(jnp.int32, shape, axis)


PLANES = 4


def both_parts(real, imag, lanes):
    count = real.shape[0] // 16
    stacked = jnp.stack(
        [real.reshape(count, 16, lanes), imag.reshape(count, 16, lanes)], axis=1
    )
    return stacked.reshape(2 * real.shape[0], lanes)


def planes_kernel(
    sizes, x_hbm, pp_hbm, ps_hbm, count_hbm, route_hbm, f_hbm, s_hbm, cap_hbm, out_ref,
    x_ref, pp_ref, ps_ref, count_ref, route_ref, cap_ref, s_ref, qsend, qall, fall, mt, mall, sel, xy, masks, gall, acc, place, ret_out, ret_in,
    local, q_send, q_recv, f_send, f_recv, m_send, m_recv, r_send, r_recv,
):
    first_count, held, rows_piece, pieces, depth, half, wide = sizes
    rows = pieces * rows_piece
    held_rows = held * rows_piece
    span = half // PLANES
    base = first_count * held
    two = 2 * wide
    me = lax.axis_index("bits")
    z = me // 4
    j = me % 4
    y = j // 2
    middle = (z == 1) | (z == 2)

    def near(pattern):
        return flip(z, pattern)

    def beside(pattern):
        return flip(j, pattern)

    def send(src, dst, send_sem, recv_sem, plane, seat):
        return pltpu.make_async_remote_copy(
            src_ref=src, dst_ref=dst, send_sem=send_sem, recv_sem=recv_sem,
            device_id={"bits": 4 * plane + seat}, device_id_type=pl.DeviceIdType.MESH,
        )

    barrier = pltpu.get_barrier_semaphore()
    for p in range(PLANES):
        for s in range(4):
            if p or s:
                pl.semaphore_signal(
                    barrier, inc=1, device_id={"bits": 4 * near(p) + beside(s)},
                    device_id_type=pl.DeviceIdType.MESH,
                )
    pairs = (
        (x_hbm, x_ref), (pp_hbm, pp_ref), (ps_hbm, ps_ref), (count_hbm, count_ref),
        (route_hbm, route_ref), (cap_hbm, cap_ref), (s_hbm, s_ref), (f_hbm, fall.at[:, :, j]),
    )
    loads = [pltpu.make_async_copy(a, b, local.at[i]) for i, (a, b) in enumerate(pairs)]
    for i in (6, 5, 0, 1, 2, 3, 4, 7):
        loads[i].start()

    line = iota((wide, two), 0)
    xy[:, :two] = jnp.where(iota((wide, two), 1) // rows_piece == line, 1.0, 0.0).astype(BF)
    reach = PLANES * wide
    line = iota((wide, reach), 0)
    xy[:, two:] = jnp.where(iota((wide, reach), 1) // 32 + base == line, 1.0, 0.0).astype(BF)
    for q in range(4):
        lane = iota((wide, reach), 0)
        col = iota((wide, reach), 1)
        inside = lane % 32
        goal = (lane // 32) * wide + (inside // 16) * (wide // 2) + 16 * q + inside % 16
        place[q * wide:(q + 1) * wide, :] = jnp.where(col == goal, 1.0, 0.0).astype(BF)

    for i in (1, 2, 3, 4, 0):
        loads[i].wait()
    eye = iota((pieces, pieces), 0) == iota((pieces, pieces), 1)

    def column(row):
        spread = jnp.broadcast_to(row, (pieces, pieces))
        return jnp.sum(jnp.where(eye, spread, 0), axis=1, keepdims=True)

    spot = iota((pieces, wide), 1)
    count = column(count_ref[...])
    table = jnp.zeros((pieces, wide), F32)
    for k in range(pp_ref.shape[0]):
        code = column(ps_ref[k:k + 1, :]) * held + column(pp_ref[k:k + 1, :])
        table = table + jnp.where((spot == code) & (count > k), 1.0, 0.0)
    for k in range(route_ref.shape[1]):
        table = table + jnp.where(spot == route_ref[:, k:k + 1] + base, 1.0, 0.0)
    table = table.astype(BF)
    for p in range(PLANES):
        qsend[p, :held_rows, :wide] = x_ref[:, p * span:(p + 1) * span]
        qsend[p, :held_rows, wide:] = x_ref[:, half + p * span:half + (p + 1) * span]
        qsend[p, held_rows:, :wide] = table
        qsend[p, held_rows:, wide:] = jnp.zeros((pieces, wide), BF)
    qall[z, j] = qsend[z]

    loads[5].wait()
    loads[6].wait()

    def times(left, part):
        return lax.dot_general(
            left, s_ref[part], (((1,), (1,)), ((), ())), preferred_element_type=F32
        )

    upper = both_parts(cap_ref[0], cap_ref[1], half)
    lower = both_parts(-cap_ref[1], cap_ref[0], half)
    closed = (times(upper, 0) + times(lower, 1)).astype(BF)
    mt[...] = closed.reshape(4, 32, half)
    mall[z, j] = mt[j]

    def m_near(t, s):
        return send(
            mt.at[beside(s)], mall.at[z, j], m_send.at[0, t, s], m_recv.at[z, y], near(t),
            beside(s),
        )

    def m_quad(s):
        side = flip(y, 1) if False else y
        return send(
            mt.at[beside(s)], mall.at[z, j], m_send.at[0, 0, s], m_recv.at[z, side], z, beside(s)
        )

    def m_pair(source, side, t, index):
        block = mall.at[source, pl.ds(2 * side, 2)]
        return send(
            block, block, m_send.at[1, t, index], m_recv.at[source, side], near(t), j
        )

    def m_arrived(source, side):
        block = mall.at[source, pl.ds(2 * side, 2)]
        send(block, block, m_send.at[0, 0, 0], m_recv.at[source, side], z, beside(1)).wait_recv()

    def q_line(t):
        return send(
            qsend.at[near(t)], qall.at[z, j], q_send.at[0, t], q_recv.at[z, j], near(t), j
        )

    def q_pass(t, s, to):
        block = qall.at[near(t), beside(s)]
        return send(
            block, block, q_send.at[to + s // 2, t], q_recv.at[near(t), beside(s)], z, beside(to)
        )

    def q_arrived(t, s):
        block = qall.at[near(t), beside(s)]
        send(
            block, block, q_send.at[0, 0], q_recv.at[near(t), beside(s)], z, beside(1)
        ).wait_recv()

    def f_copy(s):
        return send(f_hbm, fall.at[:, :, j], f_send.at[s], f_recv.at[j], z, beside(s))

    def f_pass():
        seat = beside(2)
        block = fall.at[:, :, seat]
        return send(block, block, f_send.at[0], f_recv.at[seat], z, beside(1))

    def f_arrived(seat):
        block = fall.at[:, :, seat]
        send(block, block, f_send.at[0], f_recv.at[seat], z, beside(1)).wait_recv()

    same = jnp.where(
        iota((rows_piece, two), 0) == iota((rows_piece, two), 1) % rows_piece, 1.0, 0.0
    ).astype(F32)

    group_of = iota((rows, two), 1) // held_rows

    def prepare(t):
        plane = near(t)
        tabs = jnp.concatenate(
            [qall[plane, q, held_rows:, :wide].astype(F32) for q in range(4)], axis=0
        ).astype(BF)
        spread = jnp.dot(tabs, xy[...], preferred_element_type=F32)
        for p in range(PLANES):
            masks[p, plane] = spread[:, two + p * wide:two + (p + 1) * wide]
        for q in range(4):
            wanted = spread[q * pieces:(q + 1) * pieces, :two]
            kept = jnp.broadcast_to(wanted[:, None, :], (pieces, rows_piece, two)) * same[None]
            kept = kept.reshape(rows, two)
            left = jnp.concatenate(
                [jnp.where(group_of == a, kept, 0.0).astype(BF) for a in range(first_count)],
                axis=0,
            )
            right = jnp.concatenate([qall[plane, q, :held_rows]] * first_count, axis=0)
            picked = jnp.dot(left, right, preferred_element_type=F32).astype(BF)
            for a in range(first_count):
                sel[plane, q, :, a * two:(a + 1) * two] = picked[a * rows:(a + 1) * rows]

    def gather(b, planes):
        left = jnp.concatenate([mall[p].reshape(wide, half) for p in planes], axis=0)
        for a in range(first_count):
            product = lax.dot_general(
                left, fall[a].reshape(two, half), (((1,), (1,)), ((), ())),
                preferred_element_type=F32,
            ).reshape(len(planes) * 4, 2, 16, two)
            real = product[:, 0, :, :wide] - product[:, 1, :, wide:]
            imag = product[:, 0, :, wide:] + product[:, 1, :, :wide]
            joined = jnp.stack(
                [jnp.concatenate([real, -imag], axis=-1), jnp.concatenate([imag, real], axis=-1)],
                axis=1,
            )
            gall[b, :, a * two:(a + 1) * two] = joined.reshape(len(planes) * wide, two).astype(BF)

    def part(b, planes, owner):
        lines = sel[owner].reshape(4 * rows, first_count * two)
        values = lax.dot_general(
            lines, gall[b], (((1,), (1,)), ((), ())), preferred_element_type=F32
        )
        total = None
        for u, p in enumerate(planes):
            mask = masks[p, owner].reshape(4 * pieces, 1, wide)
            mask = jnp.broadcast_to(mask, (4 * pieces, rows_piece, wide))
            term = values[:, u * wide:(u + 1) * wide] * mask.reshape(4 * rows, wide)
            total = term if total is None else total + term
        return total

    pl.semaphore_wait(barrier, 4 * PLANES - 1)
    for s in (2, 3, 1):
        m_quad(s).start()
    for s in (0, 1):
        for t in (2, 1):
            m_near(t, s).start()

    @pl.when(middle)
    def _():
        for s in (0, 1):
            m_near(3, s).start()

    for t in (3, 2, 1):
        q_line(t).start()
    for to in (2, 1):
        q_pass(0, 0, to).start()
    for s in (2, 1):
        f_copy(s).start()
    far = flip(y, 1)

    q_arrived(0, 2)
    q_pass(0, 2, 1).start()
    m_arrived(z, far)
    m_pair(z, far, 1, 0).start()

    @pl.when(middle)
    def _():
        m_pair(z, far, 3, 0).start()

    @pl.when(jnp.logical_not(middle))
    def _():
        m_pair(z, far, 2, 0).start()

    def q_spread(t):
        q_arrived(t, 0)
        for to in (2, 1):
            q_pass(t, 0, to).start()

    def q_second(t):
        q_arrived(t, 2)
        q_pass(t, 2, 1).start()

    def q_rest(t):
        q_arrived(t, 1)
        q_arrived(t, 3)

    q_spread(1)
    q_rest(0)
    prepare(0)
    q_spread(2)
    q_spread(3)

    @pl.when(middle)
    def _():
        m_arrived(near(2), y)
        m_pair(near(2), y, 1, 1).start()

    q_second(1)
    q_rest(1)
    prepare(1)

    @pl.when(middle)
    def _():
        m_arrived(near(3), far)
        m_pair(near(3), far, 1, 2).start()

    q_second(2)
    q_second(3)

    @pl.when(middle)
    def _():
        m_arrived(near(2), far)
        m_pair(near(2), far, 1, 3).start()

    f_arrived(beside(2))
    f_pass().start()
    for t in (2, 3):
        q_rest(t)
        prepare(t)
    send(
        mt.at[j], mall.at[z, beside(1)], m_send.at[0, 0, 0], m_recv.at[z, y], z, beside(1)
    ).wait_recv()
    loads[7].wait()
    f_arrived(beside(1))
    f_arrived(beside(3))
    m_arrived(near(1), y)
    m_arrived(near(1), far)
    early = (z, near(1))
    gather(0, early)

    def first_half(owner, carry):
        acc[owner] = part(0, early, owner)
        return carry

    lax.fori_loop(0, 4, first_half, 0)

    @pl.when(jnp.logical_not(middle))
    def _():
        m_arrived(near(2), y)
        m_arrived(near(2), far)
        m_arrived(near(3), far)

    m_arrived(near(3), y)
    late = (near(2), near(3))
    gather(1, late)

    def ret_copy(t, s):
        return send(
            ret_out.at[near(t), beside(s)], ret_in.at[j, z], r_send.at[s, t], r_recv.at[j, z],
            near(t), beside(s),
        )

    group = iota((32, wide), 1) // 32
    for t in (3, 2, 1, 0):
        owner = near(t)
        total = acc[owner] + part(1, late, owner)
        total = total + pltpu.roll(total, wide // 2, 1)
        total = total + pltpu.roll(total, wide // 4, 1)
        total = total.reshape(4, 4, 32, wide)
        packed = total[:, 3]
        for b in (2, 1, 0):
            packed = jnp.where(group == b, total[:, b], packed)
        ret_out[owner] = packed.astype(BF)
        for s in (3, 2, 1, 0):
            if s or t:
                ret_copy(t, s).start()
    ret_in[j, z] = ret_out[z, j]
    for t in range(PLANES):
        for s in (0, 1, 2, 3):
            if s or t:
                block = ret_in.at[beside(s), near(t)]
                send(
                    block, block, r_send.at[0, 0], r_recv.at[beside(s), near(t)], z, beside(1)
                ).wait_recv()
    left = jnp.concatenate([ret_in[q].reshape(wide, wide) for q in range(4)], axis=1)
    placed = jnp.dot(left, place[...], preferred_element_type=F32).reshape(PLANES, 32, reach)
    summed = jnp.sum(placed, axis=0)
    for b in range(4):
        out_ref[b * 32:(b + 1) * 32] = summed[:, b * wide:(b + 1) * wide]

    for s in (2, 3, 1):
        m_quad(s).wait_send()
    for s in (0, 1):
        for t in (2, 1):
            m_near(t, s).wait_send()
    m_pair(z, far, 1, 0).wait_send()

    @pl.when(middle)
    def _():
        for s in (0, 1):
            m_near(3, s).wait_send()
        m_pair(z, far, 3, 0).wait_send()
        m_pair(near(2), y, 1, 1).wait_send()
        m_pair(near(3), far, 1, 2).wait_send()
        m_pair(near(2), far, 1, 3).wait_send()

    @pl.when(jnp.logical_not(middle))
    def _():
        m_pair(z, far, 2, 0).wait_send()

    for t in (3, 2, 1):
        q_line(t).wait_send()
    for t in range(PLANES):
        for to in (2, 1):
            q_pass(t, 0, to).wait_send()
        q_pass(t, 2, 1).wait_send()
    for s in (2, 1):
        f_copy(s).wait_send()
    f_pass().wait_send()
    for s in range(4):
        for t in range(PLANES):
            if s or t:
                ret_copy(t, s).wait_send()


def on_device_planes(prefix, first_suffix, pair_prefix, pair_suffix, merge_count, suffix, routes, cap):
    pieces = pair_prefix.shape[0]
    held, rows_piece, twice_width = prefix.shape
    half = twice_width // 2
    first_count, _, depth, _ = first_suffix.shape
    wide = 2 * cap.shape[2]
    rows = pieces * rows_piece
    held_rows = held * rows_piece
    two = 2 * wide
    sizes = (first_count, held, rows_piece, pieces, depth, half, wide)
    vmem = pl.BlockSpec(memory_space=pltpu.VMEM)
    hbm = pl.BlockSpec(memory_space=pltpu.HBM)
    dma = pltpu.SemaphoreType.DMA
    out = pl.pallas_call(
        lambda *refs: planes_kernel(sizes, *refs),
        name="planes",
        out_shape=jax.ShapeDtypeStruct((rows, wide), F32),
        in_specs=[hbm] * 8,
        out_specs=vmem,
        scratch_shapes=[
            pltpu.VMEM((held_rows, twice_width), BF),
            pltpu.VMEM(pair_prefix.shape[::-1], jnp.int32),
            pltpu.VMEM(pair_prefix.shape[::-1], jnp.int32),
            pltpu.VMEM((1, pieces), jnp.int32),
            pltpu.VMEM(routes.shape, jnp.int32),
            pltpu.VMEM((2, wide // 2, half), BF),
            pltpu.VMEM((2, half, half), BF),
            pltpu.VMEM((PLANES, held_rows + pieces, two), BF),
            pltpu.VMEM((PLANES, 4, held_rows + pieces, two), BF),
            pltpu.VMEM((first_count, 2, 4, depth, half), BF),
            pltpu.VMEM((4, 32, half), BF),
            pltpu.VMEM((PLANES, 4, 32, half), BF),
            pltpu.VMEM((PLANES, 4, rows, first_count * two), BF),
            pltpu.VMEM((wide, two + PLANES * wide), BF),
            pltpu.VMEM((PLANES, PLANES, 4 * pieces, wide), F32),
            pltpu.VMEM((2, two, first_count * two), BF),
            pltpu.VMEM((PLANES, 4 * rows, wide), F32),
            pltpu.VMEM((4 * wide, PLANES * wide), BF),
            pltpu.VMEM((PLANES, 4, 32, wide), BF),
            pltpu.VMEM((4, PLANES, 32, wide), BF),
            dma((8,)), dma((4, PLANES)), dma((PLANES, 4)), dma((3,)), dma((4,)),
            dma((2, PLANES, 4)), dma((PLANES, 2)), dma((4, PLANES)), dma((4, PLANES)),
        ],
        compiler_params=pltpu.CompilerParams(
            collective_id=0, has_side_effects=True, vmem_limit_bytes=40 * 2 ** 20
        ),
    )(*[pltpu.with_memory_space_constraint(v, pltpu.HBM) for v in (
        prefix.reshape(held_rows, twice_width), pair_prefix.T, pair_suffix.T, merge_count[None],
        routes, first_suffix, suffix[0], cap.transpose(0, 2, 1),
    )])
    return out.reshape(pieces, rows_piece, wide)


def on_device(prefix, first_suffix, pair_prefix, pair_suffix, merge_count, suffix, routes, cap):
    pieces = pair_prefix.shape[0]
    listed = routes.shape[1]
    owners = lax.axis_size("bits")
    slots = min(pieces, max(2, (2 * pieces * listed + owners - 1) // owners))
    held, rows_piece, twice_width = prefix.shape
    wide = 2 * cap.shape[2]
    fits = (
        owners == 4 * PLANES and wide == 128 and pieces == 8 and rows_piece == 16
        and twice_width == 2 * PLANES * wide and first_suffix.shape[0] * held == rows_piece
        and held * rows_piece * first_suffix.shape[0] == 2 * wide and suffix.shape[0] == 1
        and owners * first_suffix.shape[2] == twice_width // 2 and owners <= wide - rows_piece
    )
    body = on_device_sparse
    if slots == pieces:
        body = on_device_planes if fits else on_device_dense
    return body(
        prefix, first_suffix, pair_prefix, pair_suffix, merge_count, suffix, routes, cap
    )


def solution(mesh):
    return jax.shard_map(
        on_device,
        mesh=mesh,
        in_specs=(
            P(("grp", "bits"), None, None),
            P("grp", None, "bits", None),
            P(("grp", "bits"), None),
            P(("grp", "bits"), None),
            P(("grp", "bits")),
            P(("grp", "bits"), None, None, None),
            P(("grp", "bits"), None),
            P(),
        ),
        out_specs=P(("grp", "bits"), None, None),
        check_vma=False,
    )
```

```python
import jax
import jax.numpy as jnp
from jax import lax
from jax.experimental import pallas as pl
from jax.experimental.pallas import tpu as pltpu
from jax.sharding import PartitionSpec as P

HIGHEST_PRECISION = lax.Precision.HIGHEST


def complex_form(blocks):
    real_part = blocks[..., 0, :, :]
    imag_part = blocks[..., 1, :, :]
    upper_half = jnp.concatenate([real_part, imag_part], axis=-1)
    lower_half = jnp.concatenate([-imag_part, real_part], axis=-1)
    return jnp.concatenate([upper_half, lower_half], axis=-2)


def on_device_sparse(prefix, first_suffix, pair_prefix, pair_suffix, merge_count, suffix, routes, cap):
    pieces = pair_prefix.shape[0]
    merges = pair_prefix.shape[1]
    held_blocks = prefix.shape[0]
    rows_piece = prefix.shape[1]
    twice_width = prefix.shape[2]
    half_width = twice_width // 2
    first_count = first_suffix.shape[0]
    listed = routes.shape[1]
    owners = lax.axis_size("bits")
    slot_count = min(pieces, max(2, (2 * pieces * listed + owners - 1) // owners))
    live_mask = lax.broadcasted_iota(jnp.int32, (pieces, merges), 1) < merge_count[:, None]
    matches = (
        pair_suffix[:, :, None] == lax.broadcasted_iota(jnp.int32, (pieces, merges, first_count), 2)
    ) & live_mask[:, :, None]
    which_block = pair_prefix[:, :, None] == lax.broadcasted_iota(
        jnp.int32, (pieces, merges, held_blocks), 2
    )
    prefix_picks = jnp.einsum(
        "ika,ikp->iap", matches.astype(jnp.float32), which_block.astype(jnp.float32)
    ).astype(jnp.bfloat16)
    selected = jnp.einsum(
        "iap,prc->airc", prefix_picks, prefix, preferred_element_type=jnp.float32
    ).astype(jnp.bfloat16)
    selected = selected.reshape(first_count, pieces * rows_piece, twice_width)
    portion = lax.all_gather(first_suffix, "bits", axis=2, tiled=True)
    count_rows = portion.shape[2]
    real_cols = lax.slice_in_dim(selected, 0, count_rows, axis=2)
    imag_cols = lax.dynamic_slice_in_dim(selected, half_width, count_rows, 2)
    left_side = jnp.concatenate([real_cols, imag_cols], axis=2)
    upper_half = jnp.concatenate([portion[:, 0], portion[:, 1]], axis=2)
    lower_half = jnp.concatenate([-portion[:, 1], portion[:, 0]], axis=2)
    right_side = jnp.concatenate([upper_half, lower_half], axis=1)
    state_rows = jnp.einsum(
        "arc,acw->rw", left_side, right_side, preferred_element_type=jnp.float32
    )
    state_rows = state_rows.astype(jnp.bfloat16).reshape(pieces, rows_piece, twice_width)
    named_by = jnp.sum(
        (routes[:, :, None] == lax.broadcasted_iota(jnp.int32, (pieces, listed, owners), 2)).astype(
            jnp.int32
        ),
        axis=1,
    )
    earlier = lax.broadcasted_iota(jnp.int32, (pieces, pieces), 0) > lax.broadcasted_iota(
        jnp.int32, (pieces, pieces), 1
    )
    slot_rank = jnp.einsum(
        "ij,jd->id", earlier.astype(jnp.float32), named_by.astype(jnp.float32),
        precision=HIGHEST_PRECISION,
    ).astype(jnp.int32)
    slot_hit = (
        slot_rank[:, :, None] == lax.broadcasted_iota(jnp.int32, (pieces, owners, slot_count), 2)
    ) & (named_by[:, :, None] > 0)
    dispatch = jnp.transpose(slot_hit, (1, 2, 0)).astype(jnp.bfloat16)
    outgoing = jnp.einsum(
        "dmi,irc->dmrc", dispatch, state_rows, preferred_element_type=jnp.float32
    ).astype(jnp.bfloat16)
    own_form = complex_form(suffix[0])
    cap_form = complex_form(cap)
    products = jnp.einsum(
        "smrc,cw->smrw",
        lax.all_to_all(outgoing, "bits", split_axis=0, concat_axis=0, tiled=True),
        own_form,
        preferred_element_type=jnp.float32,
    ).astype(jnp.bfloat16)
    capped_terms = jnp.einsum(
        "smrw,wv->smrv", products, cap_form, preferred_element_type=jnp.float32
    )
    returned = lax.all_to_all(
        capped_terms.astype(jnp.bfloat16), "bits", split_axis=0, concat_axis=0, tiled=True
    ).astype(capped_terms.dtype)
    return jnp.einsum(
        "dmi,dmrv->irv", dispatch.astype(jnp.float32), returned, precision=HIGHEST_PRECISION
    )


def weights_of(pair_prefix, pair_suffix, merge_count, held_blocks, first_count):
    pieces, merges = pair_prefix.shape
    live_mask = lax.broadcasted_iota(jnp.int32, (pieces, merges), 1) < merge_count[:, None]
    matches = (
        pair_suffix[:, :, None] == lax.broadcasted_iota(jnp.int32, (pieces, merges, first_count), 2)
    ) & live_mask[:, :, None]
    which_block = pair_prefix[:, :, None] == lax.broadcasted_iota(
        jnp.int32, (pieces, merges, held_blocks), 2
    )
    return jnp.sum(
        (matches[:, :, :, None] & which_block[:, :, None, :]).astype(jnp.float32), axis=1
    ).astype(jnp.bfloat16)


def on_device_dense(prefix, first_suffix, pair_prefix, pair_suffix, merge_count, suffix, routes, cap):
    pieces = pair_prefix.shape[0]
    held_blocks, rows_piece, twice_width = prefix.shape
    first_count = first_suffix.shape[0]
    owners = lax.axis_size("bits")
    listed = routes.shape[1]
    portion = lax.all_gather(first_suffix, "bits", axis=2, tiled=True)
    cap_form = jnp.concatenate([cap[0], cap[1]], axis=1)
    cap_turn = jnp.concatenate([-cap[1], cap[0]], axis=1)
    closed = (
        jnp.dot(suffix[0, 0], cap_form, preferred_element_type=jnp.float32)
        + jnp.dot(suffix[0, 1], cap_turn, preferred_element_type=jnp.float32)
    ).astype(jnp.bfloat16)
    closed_all = lax.all_gather(closed, "bits", axis=1, tiled=False)
    picks = weights_of(pair_prefix, pair_suffix, merge_count, held_blocks, first_count)
    selected = jnp.einsum(
        "iap,prc->airc", picks, prefix, preferred_element_type=jnp.float32
    ).astype(jnp.bfloat16)
    selected = selected.reshape(first_count, pieces * rows_piece, twice_width)
    half = twice_width // 2
    real = selected[:, :, :half]
    imag = selected[:, :, half:]
    by_real = jnp.einsum(
        "arc,acw->rw", jnp.concatenate([real, -imag], axis=2),
        portion.reshape(first_count, twice_width, half), preferred_element_type=jnp.float32,
    )
    by_imag = jnp.einsum(
        "arc,acw->rw", jnp.concatenate([imag, real], axis=2),
        portion.reshape(first_count, twice_width, half), preferred_element_type=jnp.float32,
    )
    state_real = by_real.astype(jnp.bfloat16)
    state_imag = by_imag.astype(jnp.bfloat16)
    flat = closed_all.reshape(half, -1)
    capw = cap.shape[2]
    stacked = jnp.concatenate([state_real, state_imag], axis=0)
    both = jnp.dot(stacked, flat, preferred_element_type=jnp.float32)
    both = both.reshape(2, pieces, rows_piece, owners, 2, capw)
    named = jnp.sum(
        (routes[:, :, None] == lax.broadcasted_iota(jnp.int32, (pieces, listed, owners), 2)).astype(
            jnp.float32
        ),
        axis=1,
    )
    summed = jnp.sum(both * named[None, :, None, :, None, None], axis=3)
    out_real = summed[0, :, :, 0] - summed[1, :, :, 1]
    out_imag = summed[0, :, :, 1] + summed[1, :, :, 0]
    return jnp.concatenate([out_real, out_imag], axis=-1)


BF = jnp.bfloat16
F32 = jnp.float32


def flip(value, pattern):
    bit = 1
    while bit <= pattern:
        if pattern & bit:
            value = value + bit - 2 * bit * ((value // bit) % 2)
        bit *= 2
    return value


def iota(shape, axis):
    return lax.broadcasted_iota(jnp.int32, shape, axis)


PLANES = 4


def both_parts(real, imag, lanes):
    count = real.shape[0] // 16
    stacked = jnp.stack(
        [real.reshape(count, 16, lanes), imag.reshape(count, 16, lanes)], axis=1
    )
    return stacked.reshape(2 * real.shape[0], lanes)


def planes_kernel(
    sizes, x_hbm, pp_hbm, ps_hbm, count_hbm, route_hbm, f_hbm, s_hbm, cap_hbm, out_ref,
    x_ref, pp_ref, ps_ref, count_ref, route_ref, cap_ref, s_ref, qsend, qall, fall, mt, mall, sel, xy, masks, gall, acc, place, ret_out, ret_in,
    local, q_send, q_recv, f_send, f_recv, m_send, m_recv, r_send, r_recv,
):
    first_count, held, rows_piece, pieces, depth, half, wide = sizes
    rows = pieces * rows_piece
    held_rows = held * rows_piece
    span = half // PLANES
    base = first_count * held
    two = 2 * wide
    me = lax.axis_index("bits")
    z = me // 4
    j = me % 4
    y = j // 2
    middle = (z == 1) | (z == 2)

    def near(pattern):
        return flip(z, pattern)

    def beside(pattern):
        return flip(j, pattern)

    def send(src, dst, send_sem, recv_sem, plane, seat):
        return pltpu.make_async_remote_copy(
            src_ref=src, dst_ref=dst, send_sem=send_sem, recv_sem=recv_sem,
            device_id={"bits": 4 * plane + seat}, device_id_type=pl.DeviceIdType.MESH,
        )

    barrier = pltpu.get_barrier_semaphore()
    for p in (1, 2, 3, 0):
        for s in range(4):
            if p or s:
                pl.semaphore_signal(
                    barrier, inc=1, device_id={"bits": 4 * near(p) + beside(s)},
                    device_id_type=pl.DeviceIdType.MESH,
                )
    pairs = (
        (x_hbm, x_ref), (pp_hbm, pp_ref), (ps_hbm, ps_ref), (count_hbm, count_ref),
        (route_hbm, route_ref), (cap_hbm, cap_ref), (s_hbm, s_ref), (f_hbm, fall.at[:, :, j]),
    )
    loads = [pltpu.make_async_copy(a, b, local.at[i]) for i, (a, b) in enumerate(pairs)]
    for i in (6, 5, 0, 1, 2, 3, 4, 7):
        loads[i].start()

    line = iota((wide, two), 0)
    xy[:, :two] = jnp.where(iota((wide, two), 1) // rows_piece == line, 1.0, 0.0).astype(BF)
    reach = PLANES * wide
    line = iota((wide, reach), 0)
    xy[:, two:] = jnp.where(iota((wide, reach), 1) // 32 + base == line, 1.0, 0.0).astype(BF)
    for q in range(4):
        lane = iota((wide, reach), 0)
        col = iota((wide, reach), 1)
        inside = lane % 32
        goal = (lane // 32) * wide + (inside // 16) * (wide // 2) + 16 * q + inside % 16
        place[q * wide:(q + 1) * wide, :] = jnp.where(col == goal, 1.0, 0.0).astype(BF)

    for i in (1, 2, 3, 4, 0):
        loads[i].wait()
    eye = iota((pieces, pieces), 0) == iota((pieces, pieces), 1)

    def column(row):
        spread = jnp.broadcast_to(row, (pieces, pieces))
        return jnp.sum(jnp.where(eye, spread, 0), axis=1, keepdims=True)

    spot = iota((pieces, wide), 1)
    count = column(count_ref[...])
    table = jnp.zeros((pieces, wide), F32)
    for k in range(pp_ref.shape[0]):
        code = column(ps_ref[k:k + 1, :]) * held + column(pp_ref[k:k + 1, :])
        table = table + jnp.where((spot == code) & (count > k), 1.0, 0.0)
    for k in range(route_ref.shape[1]):
        table = table + jnp.where(spot == route_ref[:, k:k + 1] + base, 1.0, 0.0)
    table = table.astype(BF)
    for p in range(PLANES):
        qsend[p, :held_rows, :wide] = x_ref[:, p * span:(p + 1) * span]
        qsend[p, :held_rows, wide:] = x_ref[:, half + p * span:half + (p + 1) * span]
        qsend[p, held_rows:, :wide] = table
        qsend[p, held_rows:, wide:] = jnp.zeros((pieces, wide), BF)
    qall[z, j] = qsend[z]

    loads[5].wait()
    loads[6].wait()

    def times(left, part):
        return lax.dot_general(
            left, s_ref[part], (((1,), (1,)), ((), ())), preferred_element_type=F32
        )

    upper = both_parts(cap_ref[0], cap_ref[1], half)
    lower = both_parts(-cap_ref[1], cap_ref[0], half)
    closed = (times(upper, 0) + times(lower, 1)).astype(BF)
    mt[...] = closed.reshape(4, 32, half)
    mall[z, j] = mt[j]

    def m_near(t, s):
        return send(
            mt.at[beside(s)], mall.at[z, j], m_send.at[0, t, s], m_recv.at[z, y], near(t),
            beside(s),
        )

    def m_quad(s):
        side = flip(y, 1) if False else y
        return send(
            mt.at[beside(s)], mall.at[z, j], m_send.at[0, 0, s], m_recv.at[z, side], z, beside(s)
        )

    def m_pair(source, side, t, index):
        block = mall.at[source, pl.ds(2 * side, 2)]
        return send(
            block, block, m_send.at[1, t, index], m_recv.at[source, side], near(t), j
        )

    def m_arrived(source, side):
        block = mall.at[source, pl.ds(2 * side, 2)]
        send(block, block, m_send.at[0, 0, 0], m_recv.at[source, side], z, beside(1)).wait_recv()

    def q_line(t):
        return send(
            qsend.at[near(t)], qall.at[z, j], q_send.at[0, t], q_recv.at[z, j], near(t), j
        )

    def q_pass(t, s, to):
        block = qall.at[near(t), beside(s)]
        return send(
            block, block, q_send.at[to + s // 2, t], q_recv.at[near(t), beside(s)], z, beside(to)
        )

    def q_arrived(t, s):
        block = qall.at[near(t), beside(s)]
        send(
            block, block, q_send.at[0, 0], q_recv.at[near(t), beside(s)], z, beside(1)
        ).wait_recv()

    cuts = [(0, first_count // 2)] + [(a, 1) for a in range(first_count // 2, first_count)]

    def f_block(i, seat):
        first, size = cuts[i]
        return fall.at[pl.ds(first, size), :, seat]

    def f_copy(s, i):
        first, size = cuts[i]
        return send(
            f_hbm.at[pl.ds(first, size)], f_block(i, j), f_send.at[s, i], f_recv.at[j, i], z,
            beside(s),
        )

    def f_pass(i):
        block = f_block(i, beside(2))
        return send(block, block, f_send.at[0, i], f_recv.at[beside(2), i], z, beside(1))

    def f_arrived(s, i):
        block = f_block(i, beside(s))
        send(block, block, f_send.at[0, i], f_recv.at[beside(s), i], z, beside(1)).wait_recv()

    same = jnp.where(
        iota((rows_piece, two), 0) == iota((rows_piece, two), 1) % rows_piece, 1.0, 0.0
    ).astype(F32)

    group_of = iota((rows, two), 1) // held_rows

    def prepare(t):
        plane = near(t)
        tabs = jnp.concatenate(
            [qall[plane, q, held_rows:, :wide].astype(F32) for q in range(4)], axis=0
        ).astype(BF)
        spread = jnp.dot(tabs, xy[...], preferred_element_type=F32)
        for p in range(PLANES):
            masks[p, plane] = spread[:, two + p * wide:two + (p + 1) * wide]
        for q in range(4):
            wanted = spread[q * pieces:(q + 1) * pieces, :two]
            kept = jnp.broadcast_to(wanted[:, None, :], (pieces, rows_piece, two)) * same[None]
            kept = kept.reshape(rows, two)
            left = jnp.concatenate(
                [jnp.where(group_of == a, kept, 0.0).astype(BF) for a in range(first_count)],
                axis=0,
            )
            right = jnp.concatenate([qall[plane, q, :held_rows]] * first_count, axis=0)
            picked = jnp.dot(left, right, preferred_element_type=F32).astype(BF)
            for a in range(first_count):
                sel[plane, q, :, a * two:(a + 1) * two] = picked[a * rows:(a + 1) * rows]

    def gather(b, planes):
        caps = jnp.concatenate([mall[p].reshape(wide, half) for p in planes], axis=0)
        split = caps.reshape(4 * len(planes), 2, 16, half)
        turned = jnp.stack([-split[:, 1], split[:, 0]], axis=1).reshape(caps.shape)
        right = jnp.concatenate(
            [jnp.concatenate([caps, turned], axis=1), jnp.concatenate([turned, -caps], axis=1)],
            axis=0,
        )
        left = jnp.concatenate(
            [fall[:, r].reshape(first_count * wide, half) for r in range(2)], axis=1
        )
        product = lax.dot_general(
            left, right, (((1,), (1,)), ((), ())), preferred_element_type=F32
        ).astype(BF)
        for a in range(first_count):
            for r in range(2):
                gall[b, a * two + r * wide:a * two + (r + 1) * wide] = product[
                    a * wide:(a + 1) * wide, r * two:(r + 1) * two
                ]

    own_pair = pl.ds(2 * (z // 2), 2)
    other_pair = pl.ds(2 - 2 * (z // 2), 2)

    def part(b, planes, pair):
        lines = sel[pair].reshape(8 * rows, first_count * two)
        values = jnp.dot(lines, gall[b], preferred_element_type=F32)
        total = None
        for u, p in enumerate(planes):
            mask = masks[p, pair].reshape(8 * pieces, 1, wide)
            mask = jnp.broadcast_to(mask, (8 * pieces, rows_piece, wide))
            term = values[:, u * wide:(u + 1) * wide] * mask.reshape(8 * rows, wide)
            total = term if total is None else total + term
        return total.reshape(2, 4 * rows, wide)

    pl.semaphore_wait(barrier, 4 * PLANES - 1)
    far = flip(y, 1)
    early = (z, near(1))

    def q_spread(t):
        q_arrived(t, 0)
        for to in (2, 1):
            q_pass(t, 0, to).start()

    def q_second(t):
        q_arrived(t, 2)
        q_pass(t, 2, 1).start()

    def q_rest(t):
        q_arrived(t, 1)
        q_arrived(t, 3)

    def first_half(pair):
        acc[pair] = part(0, early, pair)

    edge = jnp.logical_not(middle)
    for s in (2, 3):
        m_quad(s).start()
    for t in (3, 2, 1):
        q_line(t).start()
    for to in (2, 1):
        q_pass(0, 0, to).start()
    m_quad(1).start()
    q_arrived(0, 1)

    @pl.when(edge)
    def _():
        for s in (0, 1):
            m_near(2, s).start()

    @pl.when(middle)
    def _():
        for t in (1, 3):
            for s in (0, 1):
                m_near(t, s).start()

    f_copy(2, 0).start()
    for i in range(len(cuts)):
        f_copy(1, i).start()
    m_arrived(z, far)

    @pl.when(middle)
    def _():
        for t in (1, 3):
            m_pair(z, far, t, 0).start()

    @pl.when(edge)
    def _():
        m_pair(z, far, 2, 0).start()
        for s in (0, 1):
            m_near(1, s).start()
        m_pair(z, far, 1, 0).start()

    f_copy(2, 1).start()
    q_second(0)
    q_spread(1)
    for i in range(2, len(cuts)):
        f_copy(2, i).start()

    @pl.when(middle)
    def _():
        for s in (0, 1):
            m_near(2, s).start()

    q_arrived(0, 3)
    prepare(0)
    q_spread(2)
    q_spread(3)

    @pl.when(middle)
    def _():
        m_arrived(near(2), y)
        m_pair(near(2), y, 1, 1).start()

    q_second(1)
    for i in range(2):
        f_arrived(2, i)
        f_pass(i).start()
    q_rest(1)
    prepare(1)
    q_second(2)
    q_second(3)

    @pl.when(middle)
    def _():
        m_arrived(near(3), far)
        m_pair(near(3), far, 1, 2).start()
        m_arrived(near(2), far)
        m_pair(near(2), far, 1, 3).start()

    for i in range(2, len(cuts)):
        f_arrived(2, i)
        f_pass(i).start()
    send(
        mt.at[j], mall.at[z, beside(1)], m_send.at[0, 0, 0], m_recv.at[z, y], z, beside(1)
    ).wait_recv()
    loads[7].wait()
    m_arrived(near(1), y)
    m_arrived(near(1), far)
    for s in (1, 3):
        for i in range(len(cuts)):
            f_arrived(s, i)
    for t in (2, 3):
        q_rest(t)
        prepare(t)
    gather(0, early)
    first_half(own_pair)
    first_half(other_pair)

    @pl.when(jnp.logical_not(middle))
    def _():
        m_arrived(near(2), y)
        m_arrived(near(2), far)
        m_arrived(near(3), far)

    m_arrived(near(3), y)
    late = (near(2), near(3))
    gather(1, late)

    def ret_copy(t, s):
        return send(
            ret_out.at[near(t), beside(s)], ret_in.at[j, z], r_send.at[s, t], r_recv.at[j, z],
            near(t), beside(s),
        )

    group = iota((32, wide), 1) // 32
    for ends, pair in (((3, 2), other_pair), ((1, 0), own_pair)):
        total = (acc[pair] + part(1, late, pair)).reshape(8, 4, 32, wide)
        packed = None
        for k in range(4):
            mixed = total[:, (3 - k) % 4]
            for m in (2, 1, 0):
                mixed = jnp.where(group == m, total[:, (m - k) % 4], mixed)
            if k:
                mixed = pltpu.roll(mixed, wide - 32 * k, 2)
            packed = mixed if packed is None else packed + mixed
        ret_out[pair] = packed.astype(BF).reshape(2, 4, 32, wide)
        for t in ends:
            for s in (3, 2, 1, 0):
                if s or t:
                    ret_copy(t, s).start()
    ret_in[j, z] = ret_out[z, j]
    for t in range(PLANES):
        for s in (0, 1, 2, 3):
            if s or t:
                block = ret_in.at[beside(s), near(t)]
                send(
                    block, block, r_send.at[0, 0], r_recv.at[beside(s), near(t)], z, beside(1)
                ).wait_recv()
    left = jnp.concatenate([ret_in[q].reshape(wide, wide) for q in range(4)], axis=1)
    placed = jnp.dot(left, place[...], preferred_element_type=F32).reshape(PLANES, 32, reach)
    summed = jnp.sum(placed, axis=0)
    for b in range(4):
        out_ref[b * 32:(b + 1) * 32] = summed[:, b * wide:(b + 1) * wide]

    for s in (2, 3, 1):
        m_quad(s).wait_send()
    for s in (0, 1):
        for t in (2, 1):
            m_near(t, s).wait_send()
    m_pair(z, far, 1, 0).wait_send()

    @pl.when(middle)
    def _():
        for s in (0, 1):
            m_near(3, s).wait_send()
        m_pair(z, far, 3, 0).wait_send()
        m_pair(near(2), y, 1, 1).wait_send()
        m_pair(near(3), far, 1, 2).wait_send()
        m_pair(near(2), far, 1, 3).wait_send()

    @pl.when(jnp.logical_not(middle))
    def _():
        m_pair(z, far, 2, 0).wait_send()

    for t in (3, 2, 1):
        q_line(t).wait_send()
    for t in range(PLANES):
        for to in (2, 1):
            q_pass(t, 0, to).wait_send()
        q_pass(t, 2, 1).wait_send()
    for i in range(len(cuts)):
        for s in (2, 1):
            f_copy(s, i).wait_send()
        f_pass(i).wait_send()
    for s in range(4):
        for t in range(PLANES):
            if s or t:
                ret_copy(t, s).wait_send()


def on_device_planes(prefix, first_suffix, pair_prefix, pair_suffix, merge_count, suffix, routes, cap):
    pieces = pair_prefix.shape[0]
    held, rows_piece, twice_width = prefix.shape
    half = twice_width // 2
    first_count, _, depth, _ = first_suffix.shape
    wide = 2 * cap.shape[2]
    rows = pieces * rows_piece
    held_rows = held * rows_piece
    two = 2 * wide
    sizes = (first_count, held, rows_piece, pieces, depth, half, wide)
    vmem = pl.BlockSpec(memory_space=pltpu.VMEM)
    hbm = pl.BlockSpec(memory_space=pltpu.HBM)
    dma = pltpu.SemaphoreType.DMA
    out = pl.pallas_call(
        lambda *refs: planes_kernel(sizes, *refs),
        name="planes",
        out_shape=jax.ShapeDtypeStruct((rows, wide), F32),
        in_specs=[hbm] * 8,
        out_specs=vmem,
        scratch_shapes=[
            pltpu.VMEM((held_rows, twice_width), BF),
            pltpu.VMEM(pair_prefix.shape[::-1], jnp.int32),
            pltpu.VMEM(pair_prefix.shape[::-1], jnp.int32),
            pltpu.VMEM((1, pieces), jnp.int32),
            pltpu.VMEM(routes.shape, jnp.int32),
            pltpu.VMEM((2, wide // 2, half), BF),
            pltpu.VMEM((2, half, half), BF),
            pltpu.VMEM((PLANES, held_rows + pieces, two), BF),
            pltpu.VMEM((PLANES, 4, held_rows + pieces, two), BF),
            pltpu.VMEM((first_count, 2, 4, depth, half), BF),
            pltpu.VMEM((4, 32, half), BF),
            pltpu.VMEM((PLANES, 4, 32, half), BF),
            pltpu.VMEM((PLANES, 4, rows, first_count * two), BF),
            pltpu.VMEM((wide, two + PLANES * wide), BF),
            pltpu.VMEM((PLANES, PLANES, 4 * pieces, wide), F32),
            pltpu.VMEM((2, first_count * two, two), BF),
            pltpu.VMEM((PLANES, 4 * rows, wide), F32),
            pltpu.VMEM((4 * wide, PLANES * wide), BF),
            pltpu.VMEM((PLANES, 4, 32, wide), BF),
            pltpu.VMEM((4, PLANES, 32, wide), BF),
            dma((8,)), dma((4, PLANES)), dma((PLANES, 4)), dma((3, first_count)), dma((4, first_count)),
            dma((2, PLANES, 4)), dma((PLANES, 2)), dma((4, PLANES)), dma((4, PLANES)),
        ],
        compiler_params=pltpu.CompilerParams(
            collective_id=0, has_side_effects=True, vmem_limit_bytes=40 * 2 ** 20
        ),
    )(*[pltpu.with_memory_space_constraint(v, pltpu.HBM) for v in (
        prefix.reshape(held_rows, twice_width), pair_prefix.T, pair_suffix.T, merge_count[None],
        routes, first_suffix, suffix[0], cap.transpose(0, 2, 1),
    )])
    return out.reshape(pieces, rows_piece, wide)


def on_device(prefix, first_suffix, pair_prefix, pair_suffix, merge_count, suffix, routes, cap):
    pieces = pair_prefix.shape[0]
    listed = routes.shape[1]
    owners = lax.axis_size("bits")
    slots = min(pieces, max(2, (2 * pieces * listed + owners - 1) // owners))
    held, rows_piece, twice_width = prefix.shape
    wide = 2 * cap.shape[2]
    fits = (
        owners == 4 * PLANES and wide == 128 and pieces == 8 and rows_piece == 16
        and twice_width == 2 * PLANES * wide and first_suffix.shape[0] * held == rows_piece
        and held * rows_piece * first_suffix.shape[0] == 2 * wide and suffix.shape[0] == 1
        and owners * first_suffix.shape[2] == twice_width // 2 and owners <= wide - rows_piece
    )
    body = on_device_sparse
    if slots == pieces:
        body = on_device_planes if fits else on_device_dense
    return body(
        prefix, first_suffix, pair_prefix, pair_suffix, merge_count, suffix, routes, cap
    )


def solution(mesh):
    return jax.shard_map(
        on_device,
        mesh=mesh,
        in_specs=(
            P(("grp", "bits"), None, None),
            P("grp", None, "bits", None),
            P(("grp", "bits"), None),
            P(("grp", "bits"), None),
            P(("grp", "bits")),
            P(("grp", "bits"), None, None, None),
            P(("grp", "bits"), None),
            P(),
        ),
        out_specs=P(("grp", "bits"), None, None),
        check_vma=False,
    )
```

```python
import jax
import jax.numpy as jnp
from jax import lax
from jax.experimental import pallas as pl
from jax.experimental.pallas import tpu as pltpu
from jax.sharding import PartitionSpec as P

HIGHEST_PRECISION = lax.Precision.HIGHEST


def complex_form(blocks):
    real_part = blocks[..., 0, :, :]
    imag_part = blocks[..., 1, :, :]
    upper_half = jnp.concatenate([real_part, imag_part], axis=-1)
    lower_half = jnp.concatenate([-imag_part, real_part], axis=-1)
    return jnp.concatenate([upper_half, lower_half], axis=-2)


def on_device_sparse(prefix, first_suffix, pair_prefix, pair_suffix, merge_count, suffix, routes, cap):
    pieces = pair_prefix.shape[0]
    merges = pair_prefix.shape[1]
    held_blocks = prefix.shape[0]
    rows_piece = prefix.shape[1]
    twice_width = prefix.shape[2]
    half_width = twice_width // 2
    first_count = first_suffix.shape[0]
    listed = routes.shape[1]
    owners = lax.axis_size("bits")
    slot_count = min(pieces, max(2, (2 * pieces * listed + owners - 1) // owners))
    live_mask = lax.broadcasted_iota(jnp.int32, (pieces, merges), 1) < merge_count[:, None]
    matches = (
        pair_suffix[:, :, None] == lax.broadcasted_iota(jnp.int32, (pieces, merges, first_count), 2)
    ) & live_mask[:, :, None]
    which_block = pair_prefix[:, :, None] == lax.broadcasted_iota(
        jnp.int32, (pieces, merges, held_blocks), 2
    )
    prefix_picks = jnp.einsum(
        "ika,ikp->iap", matches.astype(jnp.float32), which_block.astype(jnp.float32)
    ).astype(jnp.bfloat16)
    selected = jnp.einsum(
        "iap,prc->airc", prefix_picks, prefix, preferred_element_type=jnp.float32
    ).astype(jnp.bfloat16)
    selected = selected.reshape(first_count, pieces * rows_piece, twice_width)
    portion = lax.all_gather(first_suffix, "bits", axis=2, tiled=True)
    count_rows = portion.shape[2]
    real_cols = lax.slice_in_dim(selected, 0, count_rows, axis=2)
    imag_cols = lax.dynamic_slice_in_dim(selected, half_width, count_rows, 2)
    left_side = jnp.concatenate([real_cols, imag_cols], axis=2)
    upper_half = jnp.concatenate([portion[:, 0], portion[:, 1]], axis=2)
    lower_half = jnp.concatenate([-portion[:, 1], portion[:, 0]], axis=2)
    right_side = jnp.concatenate([upper_half, lower_half], axis=1)
    state_rows = jnp.einsum(
        "arc,acw->rw", left_side, right_side, preferred_element_type=jnp.float32
    )
    state_rows = state_rows.astype(jnp.bfloat16).reshape(pieces, rows_piece, twice_width)
    named_by = jnp.sum(
        (routes[:, :, None] == lax.broadcasted_iota(jnp.int32, (pieces, listed, owners), 2)).astype(
            jnp.int32
        ),
        axis=1,
    )
    earlier = lax.broadcasted_iota(jnp.int32, (pieces, pieces), 0) > lax.broadcasted_iota(
        jnp.int32, (pieces, pieces), 1
    )
    slot_rank = jnp.einsum(
        "ij,jd->id", earlier.astype(jnp.float32), named_by.astype(jnp.float32),
        precision=HIGHEST_PRECISION,
    ).astype(jnp.int32)
    slot_hit = (
        slot_rank[:, :, None] == lax.broadcasted_iota(jnp.int32, (pieces, owners, slot_count), 2)
    ) & (named_by[:, :, None] > 0)
    dispatch = jnp.transpose(slot_hit, (1, 2, 0)).astype(jnp.bfloat16)
    outgoing = jnp.einsum(
        "dmi,irc->dmrc", dispatch, state_rows, preferred_element_type=jnp.float32
    ).astype(jnp.bfloat16)
    own_form = complex_form(suffix[0])
    cap_form = complex_form(cap)
    products = jnp.einsum(
        "smrc,cw->smrw",
        lax.all_to_all(outgoing, "bits", split_axis=0, concat_axis=0, tiled=True),
        own_form,
        preferred_element_type=jnp.float32,
    ).astype(jnp.bfloat16)
    capped_terms = jnp.einsum(
        "smrw,wv->smrv", products, cap_form, preferred_element_type=jnp.float32
    )
    returned = lax.all_to_all(
        capped_terms.astype(jnp.bfloat16), "bits", split_axis=0, concat_axis=0, tiled=True
    ).astype(capped_terms.dtype)
    return jnp.einsum(
        "dmi,dmrv->irv", dispatch.astype(jnp.float32), returned, precision=HIGHEST_PRECISION
    )


def weights_of(pair_prefix, pair_suffix, merge_count, held_blocks, first_count):
    pieces, merges = pair_prefix.shape
    live_mask = lax.broadcasted_iota(jnp.int32, (pieces, merges), 1) < merge_count[:, None]
    matches = (
        pair_suffix[:, :, None] == lax.broadcasted_iota(jnp.int32, (pieces, merges, first_count), 2)
    ) & live_mask[:, :, None]
    which_block = pair_prefix[:, :, None] == lax.broadcasted_iota(
        jnp.int32, (pieces, merges, held_blocks), 2
    )
    return jnp.sum(
        (matches[:, :, :, None] & which_block[:, :, None, :]).astype(jnp.float32), axis=1
    ).astype(jnp.bfloat16)


def on_device_dense(prefix, first_suffix, pair_prefix, pair_suffix, merge_count, suffix, routes, cap):
    pieces = pair_prefix.shape[0]
    held_blocks, rows_piece, twice_width = prefix.shape
    first_count = first_suffix.shape[0]
    owners = lax.axis_size("bits")
    listed = routes.shape[1]
    portion = lax.all_gather(first_suffix, "bits", axis=2, tiled=True)
    cap_form = jnp.concatenate([cap[0], cap[1]], axis=1)
    cap_turn = jnp.concatenate([-cap[1], cap[0]], axis=1)
    closed = (
        jnp.dot(suffix[0, 0], cap_form, preferred_element_type=jnp.float32)
        + jnp.dot(suffix[0, 1], cap_turn, preferred_element_type=jnp.float32)
    ).astype(jnp.bfloat16)
    closed_all = lax.all_gather(closed, "bits", axis=1, tiled=False)
    picks = weights_of(pair_prefix, pair_suffix, merge_count, held_blocks, first_count)
    selected = jnp.einsum(
        "iap,prc->airc", picks, prefix, preferred_element_type=jnp.float32
    ).astype(jnp.bfloat16)
    selected = selected.reshape(first_count, pieces * rows_piece, twice_width)
    half = twice_width // 2
    real = selected[:, :, :half]
    imag = selected[:, :, half:]
    by_real = jnp.einsum(
        "arc,acw->rw", jnp.concatenate([real, -imag], axis=2),
        portion.reshape(first_count, twice_width, half), preferred_element_type=jnp.float32,
    )
    by_imag = jnp.einsum(
        "arc,acw->rw", jnp.concatenate([imag, real], axis=2),
        portion.reshape(first_count, twice_width, half), preferred_element_type=jnp.float32,
    )
    state_real = by_real.astype(jnp.bfloat16)
    state_imag = by_imag.astype(jnp.bfloat16)
    flat = closed_all.reshape(half, -1)
    capw = cap.shape[2]
    stacked = jnp.concatenate([state_real, state_imag], axis=0)
    both = jnp.dot(stacked, flat, preferred_element_type=jnp.float32)
    both = both.reshape(2, pieces, rows_piece, owners, 2, capw)
    named = jnp.sum(
        (routes[:, :, None] == lax.broadcasted_iota(jnp.int32, (pieces, listed, owners), 2)).astype(
            jnp.float32
        ),
        axis=1,
    )
    summed = jnp.sum(both * named[None, :, None, :, None, None], axis=3)
    out_real = summed[0, :, :, 0] - summed[1, :, :, 1]
    out_imag = summed[0, :, :, 1] + summed[1, :, :, 0]
    return jnp.concatenate([out_real, out_imag], axis=-1)


BF = jnp.bfloat16
F32 = jnp.float32


def flip(value, pattern):
    bit = 1
    while bit <= pattern:
        if pattern & bit:
            value = value + bit - 2 * bit * ((value // bit) % 2)
        bit *= 2
    return value


def iota(shape, axis):
    return lax.broadcasted_iota(jnp.int32, shape, axis)


PLANES = 4


def both_parts(real, imag, lanes):
    count = real.shape[0] // 16
    stacked = jnp.stack(
        [real.reshape(count, 16, lanes), imag.reshape(count, 16, lanes)], axis=1
    )
    return stacked.reshape(2 * real.shape[0], lanes)


def planes_kernel(
    sizes, x_hbm, pp_hbm, ps_hbm, count_hbm, route_hbm, f_hbm, s_hbm, cap_hbm, out_ref,
    x_ref, pp_ref, ps_ref, count_ref, route_ref, cap_ref, s_ref, qsend, qall, fall, mt, mall, sel, xy, masks, gall, acc, place, ret_out, ret_in,
    local, q_send, q_recv, f_send, f_recv, m_send, m_recv, r_send, r_recv,
):
    first_count, held, rows_piece, pieces, depth, half, wide = sizes
    rows = pieces * rows_piece
    held_rows = held * rows_piece
    span = half // PLANES
    base = first_count * held
    two = 2 * wide
    me = lax.axis_index("bits")
    z = me // 4
    j = me % 4
    y = j // 2
    middle = (z == 1) | (z == 2)

    def near(pattern):
        return flip(z, pattern)

    def beside(pattern):
        return flip(j, pattern)

    def send(src, dst, send_sem, recv_sem, plane, seat):
        return pltpu.make_async_remote_copy(
            src_ref=src, dst_ref=dst, send_sem=send_sem, recv_sem=recv_sem,
            device_id={"bits": 4 * plane + seat}, device_id_type=pl.DeviceIdType.MESH,
        )

    barrier = pltpu.get_barrier_semaphore()
    for p in (1, 2, 3, 0):
        for s in range(4):
            if p or s:
                pl.semaphore_signal(
                    barrier, inc=1, device_id={"bits": 4 * near(p) + beside(s)},
                    device_id_type=pl.DeviceIdType.MESH,
                )
    pairs = (
        (x_hbm, x_ref), (pp_hbm, pp_ref), (ps_hbm, ps_ref), (count_hbm, count_ref),
        (route_hbm, route_ref), (cap_hbm, cap_ref), (s_hbm, s_ref), (f_hbm, fall.at[:, :, j]),
    )
    loads = [pltpu.make_async_copy(a, b, local.at[i]) for i, (a, b) in enumerate(pairs)]
    for i in (6, 5, 0, 1, 2, 3, 4, 7):
        loads[i].start()

    line = iota((wide, two), 0)
    xy[:, :two] = jnp.where(iota((wide, two), 1) // rows_piece == line, 1.0, 0.0).astype(BF)
    reach = PLANES * wide
    line = iota((wide, reach), 0)
    xy[:, two:] = jnp.where(iota((wide, reach), 1) // 32 + base == line, 1.0, 0.0).astype(BF)
    for q in range(4):
        lane = iota((wide, reach), 0)
        col = iota((wide, reach), 1)
        inside = lane % 32
        goal = (lane // 32) * wide + (inside // 16) * (wide // 2) + 16 * q + inside % 16
        place[q * wide:(q + 1) * wide, :] = jnp.where(col == goal, 1.0, 0.0).astype(BF)

    for i in (1, 2, 3, 4, 0):
        loads[i].wait()
    eye = iota((pieces, pieces), 0) == iota((pieces, pieces), 1)

    def column(row):
        spread = jnp.broadcast_to(row, (pieces, pieces))
        return jnp.sum(jnp.where(eye, spread, 0), axis=1, keepdims=True)

    spot = iota((pieces, wide), 1)
    count = column(count_ref[...])
    table = jnp.zeros((pieces, wide), F32)
    for k in range(pp_ref.shape[0]):
        code = column(ps_ref[k:k + 1, :]) * held + column(pp_ref[k:k + 1, :])
        table = table + jnp.where((spot == code) & (count > k), 1.0, 0.0)
    for k in range(route_ref.shape[1]):
        table = table + jnp.where(spot == route_ref[:, k:k + 1] + base, 1.0, 0.0)
    table = table.astype(BF)
    for p in range(PLANES):
        qsend[p, :held_rows, :wide] = x_ref[:, p * span:(p + 1) * span]
        qsend[p, :held_rows, wide:] = x_ref[:, half + p * span:half + (p + 1) * span]
        qsend[p, held_rows:, :wide] = table
        qsend[p, held_rows:, wide:] = jnp.zeros((pieces, wide), BF)
    qall[z, j] = qsend[z]

    loads[5].wait()
    loads[6].wait()

    def times(left, part):
        return lax.dot_general(
            left, s_ref[part], (((1,), (1,)), ((), ())), preferred_element_type=F32
        )

    upper = both_parts(cap_ref[0], cap_ref[1], half)
    lower = both_parts(-cap_ref[1], cap_ref[0], half)
    closed = (times(upper, 0) + times(lower, 1)).astype(BF)
    mt[...] = closed.reshape(4, 32, half)
    mall[z, j] = mt[j]

    def m_near(t, s):
        return send(
            mt.at[beside(s)], mall.at[z, j], m_send.at[0, t, s], m_recv.at[z, y], near(t),
            beside(s),
        )

    def m_quad(s):
        side = flip(y, 1) if False else y
        return send(
            mt.at[beside(s)], mall.at[z, j], m_send.at[0, 0, s], m_recv.at[z, side], z, beside(s)
        )

    def m_pair(source, side, t, index):
        block = mall.at[source, pl.ds(2 * side, 2)]
        return send(
            block, block, m_send.at[1, t, index], m_recv.at[source, side], near(t), j
        )

    def m_arrived(source, side):
        block = mall.at[source, pl.ds(2 * side, 2)]
        send(block, block, m_send.at[0, 0, 0], m_recv.at[source, side], z, beside(1)).wait_recv()

    def q_line(t):
        return send(
            qsend.at[near(t)], qall.at[z, j], q_send.at[0, t], q_recv.at[z, j], near(t), j
        )

    def q_pass(t, s, to):
        block = qall.at[near(t), beside(s)]
        return send(
            block, block, q_send.at[to + s // 2, t], q_recv.at[near(t), beside(s)], z, beside(to)
        )

    def q_arrived(t, s):
        block = qall.at[near(t), beside(s)]
        send(
            block, block, q_send.at[0, 0], q_recv.at[near(t), beside(s)], z, beside(1)
        ).wait_recv()

    cuts = [(0, first_count // 2)] + [(a, 1) for a in range(first_count // 2, first_count)]

    def f_block(i, seat):
        first, size = cuts[i]
        return fall.at[pl.ds(first, size), :, seat]

    def f_copy(s, i):
        first, size = cuts[i]
        return send(
            f_hbm.at[pl.ds(first, size)], f_block(i, j), f_send.at[s, i], f_recv.at[j, i], z,
            beside(s),
        )

    def f_pass(i):
        block = f_block(i, beside(2))
        return send(block, block, f_send.at[0, i], f_recv.at[beside(2), i], z, beside(1))

    def f_arrived(s, i):
        block = f_block(i, beside(s))
        send(block, block, f_send.at[0, i], f_recv.at[beside(s), i], z, beside(1)).wait_recv()

    same = jnp.where(
        iota((rows_piece, two), 0) == iota((rows_piece, two), 1) % rows_piece, 1.0, 0.0
    ).astype(F32)

    group_of = iota((rows, two), 1) // held_rows

    def prepare(t):
        plane = near(t)
        tabs = jnp.concatenate(
            [qall[plane, q, held_rows:, :wide].astype(F32) for q in range(4)], axis=0
        ).astype(BF)
        spread = jnp.dot(tabs, xy[...], preferred_element_type=F32)
        for p in range(PLANES):
            masks[p, plane] = spread[:, two + p * wide:two + (p + 1) * wide]
        for q in range(4):
            wanted = spread[q * pieces:(q + 1) * pieces, :two]
            kept = jnp.broadcast_to(wanted[:, None, :], (pieces, rows_piece, two)) * same[None]
            kept = kept.reshape(rows, two)
            left = jnp.concatenate(
                [jnp.where(group_of == a, kept, 0.0).astype(BF) for a in range(first_count)],
                axis=0,
            )
            right = jnp.concatenate([qall[plane, q, :held_rows]] * first_count, axis=0)
            picked = jnp.dot(left, right, preferred_element_type=F32).astype(BF)
            for a in range(first_count):
                sel[plane, q, :, a * two:(a + 1) * two] = picked[a * rows:(a + 1) * rows]

    def gather(b, planes):
        caps = jnp.concatenate([mall[p].reshape(wide, half) for p in planes], axis=0)
        split = caps.reshape(4 * len(planes), 2, 16, half)
        turned = jnp.stack([-split[:, 1], split[:, 0]], axis=1).reshape(caps.shape)
        right = jnp.concatenate(
            [jnp.concatenate([caps, turned], axis=1), jnp.concatenate([turned, -caps], axis=1)],
            axis=0,
        )
        left = jnp.concatenate(
            [fall[:, r].reshape(first_count * wide, half) for r in range(2)], axis=1
        )
        product = lax.dot_general(
            left, right, (((1,), (1,)), ((), ())), preferred_element_type=F32
        ).astype(BF)
        for a in range(first_count):
            for r in range(2):
                gall[b, a * two + r * wide:a * two + (r + 1) * wide] = product[
                    a * wide:(a + 1) * wide, r * two:(r + 1) * two
                ]

    def part(b, planes, owner):
        lines = sel[owner].reshape(4 * rows, first_count * two)
        values = jnp.dot(lines, gall[b], preferred_element_type=F32)
        total = None
        for u, p in enumerate(planes):
            mask = masks[p, owner].reshape(4 * pieces, 1, wide)
            mask = jnp.broadcast_to(mask, (4 * pieces, rows_piece, wide))
            term = values[:, u * wide:(u + 1) * wide] * mask.reshape(4 * rows, wide)
            total = term if total is None else total + term
        return total

    pl.semaphore_wait(barrier, 4 * PLANES - 1)
    far = flip(y, 1)
    early = (z, near(1))

    def q_spread(t):
        q_arrived(t, 0)
        for to in (2, 1):
            q_pass(t, 0, to).start()

    def q_second(t):
        q_arrived(t, 2)
        q_pass(t, 2, 1).start()

    def q_rest(t):
        q_arrived(t, 1)
        q_arrived(t, 3)

    edge = jnp.logical_not(middle)
    for s in (2, 3):
        m_quad(s).start()
    for t in (3, 2, 1):
        q_line(t).start()
    for to in (2, 1):
        q_pass(0, 0, to).start()
    m_quad(1).start()
    q_arrived(0, 1)

    @pl.when(edge)
    def _():
        for s in (0, 1):
            m_near(2, s).start()

    @pl.when(middle)
    def _():
        for t in (1, 3):
            for s in (0, 1):
                m_near(t, s).start()

    f_copy(2, 0).start()
    for i in range(len(cuts)):
        f_copy(1, i).start()
    m_arrived(z, far)

    @pl.when(middle)
    def _():
        for t in (1, 3):
            m_pair(z, far, t, 0).start()

    @pl.when(edge)
    def _():
        m_pair(z, far, 2, 0).start()
        for s in (0, 1):
            m_near(1, s).start()
        m_pair(z, far, 1, 0).start()

    f_copy(2, 1).start()
    q_second(0)
    q_spread(1)

    @pl.when(middle)
    def _():
        for s in (0, 1):
            m_near(2, s).start()

    q_arrived(0, 3)
    prepare(0)
    q_spread(2)
    q_spread(3)
    for i in range(2, len(cuts)):
        f_copy(2, i).start()

    @pl.when(middle)
    def _():
        m_arrived(near(2), y)
        m_pair(near(2), y, 1, 1).start()

    q_second(1)
    f_arrived(2, 0)
    f_pass(0).start()
    q_second(2)
    @pl.when(middle)
    def _():
        m_arrived(near(3), far)
        m_pair(near(3), far, 1, 2).start()
        m_arrived(near(2), far)
        m_pair(near(2), far, 1, 3).start()

    q_second(3)

    f_arrived(2, 1)
    f_pass(1).start()
    q_rest(1)
    prepare(1)
    q_rest(2)
    prepare(2)
    for i in range(2, len(cuts)):
        f_arrived(2, i)
        f_pass(i).start()
    q_rest(3)
    prepare(3)
    send(
        mt.at[j], mall.at[z, beside(1)], m_send.at[0, 0, 0], m_recv.at[z, y], z, beside(1)
    ).wait_recv()
    loads[7].wait()
    m_arrived(near(1), y)
    m_arrived(near(1), far)
    for s in (1, 3):
        for i in range(len(cuts)):
            f_arrived(s, i)
    gather(0, early)
    for t in (3, 2):
        acc[near(t)] = part(0, early, near(t))

    @pl.when(jnp.logical_not(middle))
    def _():
        m_arrived(near(2), y)
        m_arrived(near(2), far)
        m_arrived(near(3), far)

    m_arrived(near(3), y)
    late = (near(2), near(3))
    gather(1, late)

    def ret_copy(t, s):
        return send(
            ret_out.at[near(t), beside(s)], ret_in.at[j, z], r_send.at[s, t], r_recv.at[j, z],
            near(t), beside(s),
        )

    group = iota((32, wide), 1) // 32
    for ends in ((3, 2), (1, 0)):
        for t in ends:
            owner = near(t)
            total = acc[owner] if t > 1 else part(0, early, owner)
            total = (total + part(1, late, owner)).reshape(4, 4, 32, wide)
            packed = None
            for k in range(4):
                mixed = total[:, (3 - k) % 4]
                for m in (2, 1, 0):
                    mixed = jnp.where(group == m, total[:, (m - k) % 4], mixed)
                if k:
                    mixed = pltpu.roll(mixed, wide - 32 * k, 2)
                packed = mixed if packed is None else packed + mixed
            ret_out[owner] = packed.astype(BF)
        for t in ends:
            for s in (3, 2, 1, 0):
                if s or t:
                    ret_copy(t, s).start()
    ret_in[j, z] = ret_out[z, j]
    for t in range(PLANES):
        for s in (0, 1, 2, 3):
            if s or t:
                block = ret_in.at[beside(s), near(t)]
                send(
                    block, block, r_send.at[0, 0], r_recv.at[beside(s), near(t)], z, beside(1)
                ).wait_recv()
    left = jnp.concatenate([ret_in[q].reshape(wide, wide) for q in range(4)], axis=1)
    placed = jnp.dot(left, place[...], preferred_element_type=F32).reshape(PLANES, 32, reach)
    summed = jnp.sum(placed, axis=0)
    for b in range(4):
        out_ref[b * 32:(b + 1) * 32] = summed[:, b * wide:(b + 1) * wide]

    for s in (2, 3, 1):
        m_quad(s).wait_send()
    for s in (0, 1):
        for t in (2, 1):
            m_near(t, s).wait_send()
    m_pair(z, far, 1, 0).wait_send()

    @pl.when(middle)
    def _():
        for s in (0, 1):
            m_near(3, s).wait_send()
        m_pair(z, far, 3, 0).wait_send()
        m_pair(near(2), y, 1, 1).wait_send()
        m_pair(near(3), far, 1, 2).wait_send()
        m_pair(near(2), far, 1, 3).wait_send()

    @pl.when(jnp.logical_not(middle))
    def _():
        m_pair(z, far, 2, 0).wait_send()

    for t in (3, 2, 1):
        q_line(t).wait_send()
    for t in range(PLANES):
        for to in (2, 1):
            q_pass(t, 0, to).wait_send()
        q_pass(t, 2, 1).wait_send()
    for i in range(len(cuts)):
        for s in (2, 1):
            f_copy(s, i).wait_send()
        f_pass(i).wait_send()
    for s in range(4):
        for t in range(PLANES):
            if s or t:
                ret_copy(t, s).wait_send()


def on_device_planes(prefix, first_suffix, pair_prefix, pair_suffix, merge_count, suffix, routes, cap):
    pieces = pair_prefix.shape[0]
    held, rows_piece, twice_width = prefix.shape
    half = twice_width // 2
    first_count, _, depth, _ = first_suffix.shape
    wide = 2 * cap.shape[2]
    rows = pieces * rows_piece
    held_rows = held * rows_piece
    two = 2 * wide
    sizes = (first_count, held, rows_piece, pieces, depth, half, wide)
    vmem = pl.BlockSpec(memory_space=pltpu.VMEM)
    hbm = pl.BlockSpec(memory_space=pltpu.HBM)
    dma = pltpu.SemaphoreType.DMA
    out = pl.pallas_call(
        lambda *refs: planes_kernel(sizes, *refs),
        name="planes",
        out_shape=jax.ShapeDtypeStruct((rows, wide), F32),
        in_specs=[hbm] * 8,
        out_specs=vmem,
        scratch_shapes=[
            pltpu.VMEM((held_rows, twice_width), BF),
            pltpu.VMEM(pair_prefix.shape[::-1], jnp.int32),
            pltpu.VMEM(pair_prefix.shape[::-1], jnp.int32),
            pltpu.VMEM((1, pieces), jnp.int32),
            pltpu.VMEM(routes.shape, jnp.int32),
            pltpu.VMEM((2, wide // 2, half), BF),
            pltpu.VMEM((2, half, half), BF),
            pltpu.VMEM((PLANES, held_rows + pieces, two), BF),
            pltpu.VMEM((PLANES, 4, held_rows + pieces, two), BF),
            pltpu.VMEM((first_count, 2, 4, depth, half), BF),
            pltpu.VMEM((4, 32, half), BF),
            pltpu.VMEM((PLANES, 4, 32, half), BF),
            pltpu.VMEM((PLANES, 4, rows, first_count * two), BF),
            pltpu.VMEM((wide, two + PLANES * wide), BF),
            pltpu.VMEM((PLANES, PLANES, 4 * pieces, wide), F32),
            pltpu.VMEM((2, first_count * two, two), BF),
            pltpu.VMEM((PLANES, 4 * rows, wide), F32),
            pltpu.VMEM((4 * wide, PLANES * wide), BF),
            pltpu.VMEM((PLANES, 4, 32, wide), BF),
            pltpu.VMEM((4, PLANES, 32, wide), BF),
            dma((8,)), dma((4, PLANES)), dma((PLANES, 4)), dma((3, first_count)), dma((4, first_count)),
            dma((2, PLANES, 4)), dma((PLANES, 2)), dma((4, PLANES)), dma((4, PLANES)),
        ],
        compiler_params=pltpu.CompilerParams(
            collective_id=0, has_side_effects=True, vmem_limit_bytes=40 * 2 ** 20
        ),
    )(*[pltpu.with_memory_space_constraint(v, pltpu.HBM) for v in (
        prefix.reshape(held_rows, twice_width), pair_prefix.T, pair_suffix.T, merge_count[None],
        routes, first_suffix, suffix[0], cap.transpose(0, 2, 1),
    )])
    return out.reshape(pieces, rows_piece, wide)


def on_device(prefix, first_suffix, pair_prefix, pair_suffix, merge_count, suffix, routes, cap):
    pieces = pair_prefix.shape[0]
    listed = routes.shape[1]
    owners = lax.axis_size("bits")
    slots = min(pieces, max(2, (2 * pieces * listed + owners - 1) // owners))
    held, rows_piece, twice_width = prefix.shape
    wide = 2 * cap.shape[2]
    fits = (
        owners == 4 * PLANES and wide == 128 and pieces == 8 and rows_piece == 16
        and twice_width == 2 * PLANES * wide and first_suffix.shape[0] * held == rows_piece
        and held * rows_piece * first_suffix.shape[0] == 2 * wide and suffix.shape[0] == 1
        and owners * first_suffix.shape[2] == twice_width // 2 and owners <= wide - rows_piece
    )
    body = on_device_sparse
    if slots == pieces:
        body = on_device_planes if fits else on_device_dense
    return body(
        prefix, first_suffix, pair_prefix, pair_suffix, merge_count, suffix, routes, cap
    )


def solution(mesh):
    return jax.shard_map(
        on_device,
        mesh=mesh,
        in_specs=(
            P(("grp", "bits"), None, None),
            P("grp", None, "bits", None),
            P(("grp", "bits"), None),
            P(("grp", "bits"), None),
            P(("grp", "bits")),
            P(("grp", "bits"), None, None, None),
            P(("grp", "bits"), None),
            P(),
        ),
        out_specs=P(("grp", "bits"), None, None),
        check_vma=False,
    )
```

```python
import jax
import jax.numpy as jnp
from jax import lax
from jax.experimental import pallas as pl
from jax.experimental.pallas import tpu as pltpu
from jax.sharding import PartitionSpec as P

HIGHEST_PRECISION = lax.Precision.HIGHEST


def complex_form(blocks):
    real_part = blocks[..., 0, :, :]
    imag_part = blocks[..., 1, :, :]
    upper_half = jnp.concatenate([real_part, imag_part], axis=-1)
    lower_half = jnp.concatenate([-imag_part, real_part], axis=-1)
    return jnp.concatenate([upper_half, lower_half], axis=-2)


def on_device_sparse(prefix, first_suffix, pair_prefix, pair_suffix, merge_count, suffix, routes, cap):
    pieces = pair_prefix.shape[0]
    merges = pair_prefix.shape[1]
    held_blocks = prefix.shape[0]
    rows_piece = prefix.shape[1]
    twice_width = prefix.shape[2]
    half_width = twice_width // 2
    first_count = first_suffix.shape[0]
    listed = routes.shape[1]
    owners = lax.axis_size("bits")
    slot_count = min(pieces, max(2, (2 * pieces * listed + owners - 1) // owners))
    live_mask = lax.broadcasted_iota(jnp.int32, (pieces, merges), 1) < merge_count[:, None]
    matches = (
        pair_suffix[:, :, None] == lax.broadcasted_iota(jnp.int32, (pieces, merges, first_count), 2)
    ) & live_mask[:, :, None]
    which_block = pair_prefix[:, :, None] == lax.broadcasted_iota(
        jnp.int32, (pieces, merges, held_blocks), 2
    )
    prefix_picks = jnp.einsum(
        "ika,ikp->iap", matches.astype(jnp.float32), which_block.astype(jnp.float32)
    ).astype(jnp.bfloat16)
    selected = jnp.einsum(
        "iap,prc->airc", prefix_picks, prefix, preferred_element_type=jnp.float32
    ).astype(jnp.bfloat16)
    selected = selected.reshape(first_count, pieces * rows_piece, twice_width)
    portion = lax.all_gather(first_suffix, "bits", axis=2, tiled=True)
    count_rows = portion.shape[2]
    real_cols = lax.slice_in_dim(selected, 0, count_rows, axis=2)
    imag_cols = lax.dynamic_slice_in_dim(selected, half_width, count_rows, 2)
    left_side = jnp.concatenate([real_cols, imag_cols], axis=2)
    upper_half = jnp.concatenate([portion[:, 0], portion[:, 1]], axis=2)
    lower_half = jnp.concatenate([-portion[:, 1], portion[:, 0]], axis=2)
    right_side = jnp.concatenate([upper_half, lower_half], axis=1)
    state_rows = jnp.einsum(
        "arc,acw->rw", left_side, right_side, preferred_element_type=jnp.float32
    )
    state_rows = state_rows.astype(jnp.bfloat16).reshape(pieces, rows_piece, twice_width)
    named_by = jnp.sum(
        (routes[:, :, None] == lax.broadcasted_iota(jnp.int32, (pieces, listed, owners), 2)).astype(
            jnp.int32
        ),
        axis=1,
    )
    earlier = lax.broadcasted_iota(jnp.int32, (pieces, pieces), 0) > lax.broadcasted_iota(
        jnp.int32, (pieces, pieces), 1
    )
    slot_rank = jnp.einsum(
        "ij,jd->id", earlier.astype(jnp.float32), named_by.astype(jnp.float32),
        precision=HIGHEST_PRECISION,
    ).astype(jnp.int32)
    slot_hit = (
        slot_rank[:, :, None] == lax.broadcasted_iota(jnp.int32, (pieces, owners, slot_count), 2)
    ) & (named_by[:, :, None] > 0)
    dispatch = jnp.transpose(slot_hit, (1, 2, 0)).astype(jnp.bfloat16)
    outgoing = jnp.einsum(
        "dmi,irc->dmrc", dispatch, state_rows, preferred_element_type=jnp.float32
    ).astype(jnp.bfloat16)
    own_form = complex_form(suffix[0])
    cap_form = complex_form(cap)
    products = jnp.einsum(
        "smrc,cw->smrw",
        lax.all_to_all(outgoing, "bits", split_axis=0, concat_axis=0, tiled=True),
        own_form,
        preferred_element_type=jnp.float32,
    ).astype(jnp.bfloat16)
    capped_terms = jnp.einsum(
        "smrw,wv->smrv", products, cap_form, preferred_element_type=jnp.float32
    )
    returned = lax.all_to_all(
        capped_terms.astype(jnp.bfloat16), "bits", split_axis=0, concat_axis=0, tiled=True
    ).astype(capped_terms.dtype)
    return jnp.einsum(
        "dmi,dmrv->irv", dispatch.astype(jnp.float32), returned, precision=HIGHEST_PRECISION
    )


def weights_of(pair_prefix, pair_suffix, merge_count, held_blocks, first_count):
    pieces, merges = pair_prefix.shape
    live_mask = lax.broadcasted_iota(jnp.int32, (pieces, merges), 1) < merge_count[:, None]
    matches = (
        pair_suffix[:, :, None] == lax.broadcasted_iota(jnp.int32, (pieces, merges, first_count), 2)
    ) & live_mask[:, :, None]
    which_block = pair_prefix[:, :, None] == lax.broadcasted_iota(
        jnp.int32, (pieces, merges, held_blocks), 2
    )
    return jnp.sum(
        (matches[:, :, :, None] & which_block[:, :, None, :]).astype(jnp.float32), axis=1
    ).astype(jnp.bfloat16)


def on_device_dense(prefix, first_suffix, pair_prefix, pair_suffix, merge_count, suffix, routes, cap):
    pieces = pair_prefix.shape[0]
    held_blocks, rows_piece, twice_width = prefix.shape
    first_count = first_suffix.shape[0]
    owners = lax.axis_size("bits")
    listed = routes.shape[1]
    portion = lax.all_gather(first_suffix, "bits", axis=2, tiled=True)
    cap_form = jnp.concatenate([cap[0], cap[1]], axis=1)
    cap_turn = jnp.concatenate([-cap[1], cap[0]], axis=1)
    closed = (
        jnp.dot(suffix[0, 0], cap_form, preferred_element_type=jnp.float32)
        + jnp.dot(suffix[0, 1], cap_turn, preferred_element_type=jnp.float32)
    ).astype(jnp.bfloat16)
    closed_all = lax.all_gather(closed, "bits", axis=1, tiled=False)
    picks = weights_of(pair_prefix, pair_suffix, merge_count, held_blocks, first_count)
    selected = jnp.einsum(
        "iap,prc->airc", picks, prefix, preferred_element_type=jnp.float32
    ).astype(jnp.bfloat16)
    selected = selected.reshape(first_count, pieces * rows_piece, twice_width)
    half = twice_width // 2
    real = selected[:, :, :half]
    imag = selected[:, :, half:]
    by_real = jnp.einsum(
        "arc,acw->rw", jnp.concatenate([real, -imag], axis=2),
        portion.reshape(first_count, twice_width, half), preferred_element_type=jnp.float32,
    )
    by_imag = jnp.einsum(
        "arc,acw->rw", jnp.concatenate([imag, real], axis=2),
        portion.reshape(first_count, twice_width, half), preferred_element_type=jnp.float32,
    )
    state_real = by_real.astype(jnp.bfloat16)
    state_imag = by_imag.astype(jnp.bfloat16)
    flat = closed_all.reshape(half, -1)
    capw = cap.shape[2]
    stacked = jnp.concatenate([state_real, state_imag], axis=0)
    both = jnp.dot(stacked, flat, preferred_element_type=jnp.float32)
    both = both.reshape(2, pieces, rows_piece, owners, 2, capw)
    named = jnp.sum(
        (routes[:, :, None] == lax.broadcasted_iota(jnp.int32, (pieces, listed, owners), 2)).astype(
            jnp.float32
        ),
        axis=1,
    )
    summed = jnp.sum(both * named[None, :, None, :, None, None], axis=3)
    out_real = summed[0, :, :, 0] - summed[1, :, :, 1]
    out_imag = summed[0, :, :, 1] + summed[1, :, :, 0]
    return jnp.concatenate([out_real, out_imag], axis=-1)


BF = jnp.bfloat16
F32 = jnp.float32


def flip(value, pattern):
    bit = 1
    while bit <= pattern:
        if pattern & bit:
            value = value + bit - 2 * bit * ((value // bit) % 2)
        bit *= 2
    return value


def iota(shape, axis):
    return lax.broadcasted_iota(jnp.int32, shape, axis)


PLANES = 4


def both_parts(real, imag, lanes):
    count = real.shape[0] // 16
    stacked = jnp.stack(
        [real.reshape(count, 16, lanes), imag.reshape(count, 16, lanes)], axis=1
    )
    return stacked.reshape(2 * real.shape[0], lanes)


def planes_kernel(
    sizes, x_hbm, pp_hbm, ps_hbm, count_hbm, route_hbm, f_hbm, s_hbm, cap_hbm, out_ref,
    x_ref, pp_ref, ps_ref, count_ref, route_ref, cap_ref, s_ref, qsend, qall, fall, mt, mall, sel, xy, masks, gall, acc, place, ret_out, ret_in,
    local, q_send, q_recv, f_send, f_recv, m_send, m_recv, r_send, r_recv,
):
    first_count, held, rows_piece, pieces, depth, half, wide = sizes
    rows = pieces * rows_piece
    held_rows = held * rows_piece
    span = half // PLANES
    base = first_count * held
    two = 2 * wide
    me = lax.axis_index("bits")
    z = me // 4
    j = me % 4
    y = j // 2
    middle = (z == 1) | (z == 2)

    def near(pattern):
        return flip(z, pattern)

    def beside(pattern):
        return flip(j, pattern)

    def send(src, dst, send_sem, recv_sem, plane, seat):
        return pltpu.make_async_remote_copy(
            src_ref=src, dst_ref=dst, send_sem=send_sem, recv_sem=recv_sem,
            device_id={"bits": 4 * plane + seat}, device_id_type=pl.DeviceIdType.MESH,
        )

    barrier = pltpu.get_barrier_semaphore()
    for p in (1, 2, 3, 0):
        for s in range(4):
            if p or s:
                pl.semaphore_signal(
                    barrier, inc=1, device_id={"bits": 4 * near(p) + beside(s)},
                    device_id_type=pl.DeviceIdType.MESH,
                )
    pairs = (
        (x_hbm, x_ref), (pp_hbm, pp_ref), (ps_hbm, ps_ref), (count_hbm, count_ref),
        (route_hbm, route_ref), (cap_hbm, cap_ref), (s_hbm, s_ref), (f_hbm, fall.at[:, :, j]),
    )
    loads = [pltpu.make_async_copy(a, b, local.at[i]) for i, (a, b) in enumerate(pairs)]
    for i in (6, 5, 0, 1, 2, 3, 4, 7):
        loads[i].start()

    line = iota((wide, two), 0)
    xy[:, :two] = jnp.where(iota((wide, two), 1) // rows_piece == line, 1.0, 0.0).astype(BF)
    reach = PLANES * wide
    line = iota((wide, reach), 0)
    xy[:, two:] = jnp.where(iota((wide, reach), 1) // 32 + base == line, 1.0, 0.0).astype(BF)
    for q in range(4):
        lane = iota((wide, reach), 0)
        col = iota((wide, reach), 1)
        inside = lane % 32
        goal = (lane // 32) * wide + (inside // 16) * (wide // 2) + 16 * q + inside % 16
        place[q * wide:(q + 1) * wide, :] = jnp.where(col == goal, 1.0, 0.0).astype(BF)

    for i in (1, 2, 3, 4, 0):
        loads[i].wait()
    eye = iota((pieces, pieces), 0) == iota((pieces, pieces), 1)

    def column(row):
        spread = jnp.broadcast_to(row, (pieces, pieces))
        return jnp.sum(jnp.where(eye, spread, 0), axis=1, keepdims=True)

    spot = iota((pieces, wide), 1)
    count = column(count_ref[...])
    table = jnp.zeros((pieces, wide), F32)
    for k in range(pp_ref.shape[0]):
        code = column(ps_ref[k:k + 1, :]) * held + column(pp_ref[k:k + 1, :])
        table = table + jnp.where((spot == code) & (count > k), 1.0, 0.0)
    for k in range(route_ref.shape[1]):
        table = table + jnp.where(spot == route_ref[:, k:k + 1] + base, 1.0, 0.0)
    table = table.astype(BF)
    for p in range(PLANES):
        qsend[p, :held_rows, :wide] = x_ref[:, p * span:(p + 1) * span]
        qsend[p, :held_rows, wide:] = x_ref[:, half + p * span:half + (p + 1) * span]
        qsend[p, held_rows:, :wide] = table
        qsend[p, held_rows:, wide:] = jnp.zeros((pieces, wide), BF)
    qall[z, j] = qsend[z]

    loads[5].wait()
    loads[6].wait()

    def times(left, part):
        return lax.dot_general(
            left, s_ref[part], (((1,), (1,)), ((), ())), preferred_element_type=F32
        )

    upper = both_parts(cap_ref[0], cap_ref[1], half)
    lower = both_parts(-cap_ref[1], cap_ref[0], half)
    closed = (times(upper, 0) + times(lower, 1)).astype(BF)
    mt[...] = closed.reshape(4, 32, half)
    mall[z, j] = mt[j]

    def m_near(t, s):
        return send(
            mt.at[beside(s)], mall.at[z, j], m_send.at[0, t, s], m_recv.at[z, y], near(t),
            beside(s),
        )

    def m_quad(s):
        side = flip(y, 1) if False else y
        return send(
            mt.at[beside(s)], mall.at[z, j], m_send.at[0, 0, s], m_recv.at[z, side], z, beside(s)
        )

    def m_pair(source, side, t, index):
        block = mall.at[source, pl.ds(2 * side, 2)]
        return send(
            block, block, m_send.at[1, t, index], m_recv.at[source, side], near(t), j
        )

    def m_arrived(source, side):
        block = mall.at[source, pl.ds(2 * side, 2)]
        send(block, block, m_send.at[0, 0, 0], m_recv.at[source, side], z, beside(1)).wait_recv()

    def q_line(t):
        return send(
            qsend.at[near(t)], qall.at[z, j], q_send.at[0, t], q_recv.at[z, j], near(t), j
        )

    def q_pass(t, s, to):
        block = qall.at[near(t), beside(s)]
        return send(
            block, block, q_send.at[to + s // 2, t], q_recv.at[near(t), beside(s)], z, beside(to)
        )

    def q_arrived(t, s):
        block = qall.at[near(t), beside(s)]
        send(
            block, block, q_send.at[0, 0], q_recv.at[near(t), beside(s)], z, beside(1)
        ).wait_recv()

    cuts = [(0, first_count // 2)] + [(a, 1) for a in range(first_count // 2, first_count)]

    def f_block(i, seat):
        first, size = cuts[i]
        return fall.at[pl.ds(first, size), :, seat]

    def f_copy(s, i):
        first, size = cuts[i]
        return send(
            f_hbm.at[pl.ds(first, size)], f_block(i, j), f_send.at[s, i], f_recv.at[j, i], z,
            beside(s),
        )

    def f_pass(i):
        block = f_block(i, beside(2))
        return send(block, block, f_send.at[0, i], f_recv.at[beside(2), i], z, beside(1))

    def f_arrived(s, i):
        block = f_block(i, beside(s))
        send(block, block, f_send.at[0, i], f_recv.at[beside(s), i], z, beside(1)).wait_recv()

    same = jnp.where(
        iota((rows_piece, two), 0) == iota((rows_piece, two), 1) % rows_piece, 1.0, 0.0
    ).astype(F32)

    group_of = [
        jnp.where(iota((rows, two), 1) // held_rows == a, 1.0, 0.0).astype(BF)
        for a in range(first_count)
    ]

    def prepare(t):
        plane = near(t)
        tabs = jnp.concatenate(
            [qall[plane, q, held_rows:, :wide].astype(F32) for q in range(4)], axis=0
        ).astype(BF)
        spread = jnp.dot(tabs, xy[...], preferred_element_type=F32)
        for p in range(PLANES):
            masks[p, plane] = spread[:, two + p * wide:two + (p + 1) * wide]
        for q in range(4):
            wanted = spread[q * pieces:(q + 1) * pieces, :two]
            kept = jnp.broadcast_to(wanted[:, None, :], (pieces, rows_piece, two)) * same[None]
            kept = kept.reshape(rows, two).astype(BF)
            left = jnp.concatenate([kept * group_of[a] for a in range(first_count)], axis=0)
            right = jnp.concatenate([qall[plane, q, :held_rows]] * first_count, axis=0)
            picked = jnp.dot(left, right, preferred_element_type=F32).astype(BF)
            for a in range(first_count):
                sel[plane, q, :, a * two:(a + 1) * two] = picked[a * rows:(a + 1) * rows]

    def gather(b, planes):
        caps = jnp.concatenate([mall[p].reshape(wide, half) for p in planes], axis=0)
        split = caps.reshape(4 * len(planes), 2, 16, half)
        turned = jnp.stack([-split[:, 1], split[:, 0]], axis=1).reshape(caps.shape)
        right = jnp.concatenate(
            [jnp.concatenate([caps, turned], axis=1), jnp.concatenate([turned, -caps], axis=1)],
            axis=0,
        )
        left = jnp.concatenate(
            [fall[:, r].reshape(first_count * wide, half) for r in range(2)], axis=1
        )
        product = lax.dot_general(
            left, right, (((1,), (1,)), ((), ())), preferred_element_type=F32
        ).astype(BF)
        for a in range(first_count):
            for r in range(2):
                gall[b, a * two + r * wide:a * two + (r + 1) * wide] = product[
                    a * wide:(a + 1) * wide, r * two:(r + 1) * two
                ]

    def part(b, planes, owner):
        lines = sel[owner].reshape(4 * rows, first_count * two)
        values = jnp.dot(lines, gall[b], preferred_element_type=F32)
        total = None
        for u, p in enumerate(planes):
            mask = masks[p, owner].reshape(4 * pieces, 1, wide)
            mask = jnp.broadcast_to(mask, (4 * pieces, rows_piece, wide))
            term = values[:, u * wide:(u + 1) * wide] * mask.reshape(4 * rows, wide)
            total = term if total is None else total + term
        return total

    pl.semaphore_wait(barrier, 4 * PLANES - 1)
    far = flip(y, 1)
    early = (z, near(1))

    def q_spread(t):
        q_arrived(t, 0)
        for to in (2, 1):
            q_pass(t, 0, to).start()

    def q_second(t):
        q_arrived(t, 2)
        q_pass(t, 2, 1).start()

    def q_rest(t):
        q_arrived(t, 1)
        q_arrived(t, 3)

    edge = jnp.logical_not(middle)
    for s in (2, 3):
        m_quad(s).start()
    for t in (3, 2, 1):
        q_line(t).start()
    for to in (2, 1):
        q_pass(0, 0, to).start()
    m_quad(1).start()
    q_arrived(0, 1)

    @pl.when(edge)
    def _():
        for s in (0, 1):
            m_near(2, s).start()

    @pl.when(middle)
    def _():
        for s in (0, 1):
            m_near(1, s).start()

    f_copy(2, 0).start()
    for i in range(len(cuts)):
        f_copy(1, i).start()
    m_arrived(z, far)

    @pl.when(middle)
    def _():
        for t in (1, 3):
            m_pair(z, far, t, 0).start()

    @pl.when(edge)
    def _():
        m_pair(z, far, 2, 0).start()
        for s in (0, 1):
            m_near(1, s).start()
        m_pair(z, far, 1, 0).start()

    f_copy(2, 1).start()
    q_second(0)
    q_spread(1)

    @pl.when(middle)
    def _():
        for t in (2, 3):
            for s in (0, 1):
                m_near(t, s).start()

    q_arrived(0, 3)
    prepare(0)
    q_spread(2)
    q_spread(3)
    for i in range(2, len(cuts)):
        f_copy(2, i).start()

    @pl.when(middle)
    def _():
        m_arrived(near(2), y)
        m_pair(near(2), y, 1, 1).start()

    q_second(1)

    @pl.when(middle)
    def _():
        m_arrived(near(2), far)
        m_pair(near(2), far, 1, 3).start()

    f_arrived(2, 0)
    f_pass(0).start()
    q_second(2)
    @pl.when(middle)
    def _():
        m_arrived(near(3), far)
        m_pair(near(3), far, 1, 2).start()

    q_second(3)

    f_arrived(2, 1)
    f_pass(1).start()
    q_rest(1)
    prepare(1)
    q_rest(2)
    prepare(2)
    for i in range(2, len(cuts)):
        f_arrived(2, i)
        f_pass(i).start()
    q_rest(3)
    prepare(3)
    send(
        mt.at[j], mall.at[z, beside(1)], m_send.at[0, 0, 0], m_recv.at[z, y], z, beside(1)
    ).wait_recv()
    loads[7].wait()
    m_arrived(near(1), y)
    m_arrived(near(1), far)
    for s in (1, 3):
        for i in range(len(cuts)):
            f_arrived(s, i)
    gather(0, early)
    for t in (3, 2):
        acc[near(t)] = part(0, early, near(t))

    @pl.when(jnp.logical_not(middle))
    def _():
        m_arrived(near(2), y)
        m_arrived(near(2), far)
        m_arrived(near(3), far)

    m_arrived(near(3), y)
    late = (near(2), near(3))
    gather(1, late)

    def ret_copy(t, s):
        return send(
            ret_out.at[near(t), beside(s)], ret_in.at[j, z], r_send.at[s, t], r_recv.at[j, z],
            near(t), beside(s),
        )

    group = iota((32, wide), 1) // 32
    for ends in ((3, 2), (1, 0)):
        for t in ends:
            owner = near(t)
            total = acc[owner] if t > 1 else part(0, early, owner)
            total = (total + part(1, late, owner)).reshape(4, 4, 32, wide)
            packed = None
            for k in range(4):
                mixed = total[:, (3 - k) % 4]
                for m in (2, 1, 0):
                    mixed = jnp.where(group == m, total[:, (m - k) % 4], mixed)
                if k:
                    mixed = pltpu.roll(mixed, wide - 32 * k, 2)
                packed = mixed if packed is None else packed + mixed
            ret_out[owner] = packed.astype(BF)
        for t in ends:
            for s in (3, 2, 1, 0):
                if s or t:
                    ret_copy(t, s).start()
    ret_in[j, z] = ret_out[z, j]
    for t in range(PLANES):
        for s in (0, 1, 2, 3):
            if s or t:
                block = ret_in.at[beside(s), near(t)]
                send(
                    block, block, r_send.at[0, 0], r_recv.at[beside(s), near(t)], z, beside(1)
                ).wait_recv()
    left = jnp.concatenate([ret_in[q].reshape(wide, wide) for q in range(4)], axis=1)
    placed = jnp.dot(left, place[...], preferred_element_type=F32).reshape(PLANES, 32, reach)
    summed = jnp.sum(placed, axis=0)
    for b in range(4):
        out_ref[b * 32:(b + 1) * 32] = summed[:, b * wide:(b + 1) * wide]

    for s in (2, 3, 1):
        m_quad(s).wait_send()
    for s in (0, 1):
        for t in (2, 1):
            m_near(t, s).wait_send()
    m_pair(z, far, 1, 0).wait_send()

    @pl.when(middle)
    def _():
        for s in (0, 1):
            m_near(3, s).wait_send()
        m_pair(z, far, 3, 0).wait_send()
        m_pair(near(2), y, 1, 1).wait_send()
        m_pair(near(3), far, 1, 2).wait_send()
        m_pair(near(2), far, 1, 3).wait_send()

    @pl.when(jnp.logical_not(middle))
    def _():
        m_pair(z, far, 2, 0).wait_send()

    for t in (3, 2, 1):
        q_line(t).wait_send()
    for t in range(PLANES):
        for to in (2, 1):
            q_pass(t, 0, to).wait_send()
        q_pass(t, 2, 1).wait_send()
    for i in range(len(cuts)):
        for s in (2, 1):
            f_copy(s, i).wait_send()
        f_pass(i).wait_send()
    for s in range(4):
        for t in range(PLANES):
            if s or t:
                ret_copy(t, s).wait_send()


def on_device_planes(prefix, first_suffix, pair_prefix, pair_suffix, merge_count, suffix, routes, cap):
    pieces = pair_prefix.shape[0]
    held, rows_piece, twice_width = prefix.shape
    half = twice_width // 2
    first_count, _, depth, _ = first_suffix.shape
    wide = 2 * cap.shape[2]
    rows = pieces * rows_piece
    held_rows = held * rows_piece
    two = 2 * wide
    sizes = (first_count, held, rows_piece, pieces, depth, half, wide)
    vmem = pl.BlockSpec(memory_space=pltpu.VMEM)
    hbm = pl.BlockSpec(memory_space=pltpu.HBM)
    dma = pltpu.SemaphoreType.DMA
    out = pl.pallas_call(
        lambda *refs: planes_kernel(sizes, *refs),
        name="planes",
        out_shape=jax.ShapeDtypeStruct((rows, wide), F32),
        in_specs=[hbm] * 8,
        out_specs=vmem,
        scratch_shapes=[
            pltpu.VMEM((held_rows, twice_width), BF),
            pltpu.VMEM(pair_prefix.shape[::-1], jnp.int32),
            pltpu.VMEM(pair_prefix.shape[::-1], jnp.int32),
            pltpu.VMEM((1, pieces), jnp.int32),
            pltpu.VMEM(routes.shape, jnp.int32),
            pltpu.VMEM((2, wide // 2, half), BF),
            pltpu.VMEM((2, half, half), BF),
            pltpu.VMEM((PLANES, held_rows + pieces, two), BF),
            pltpu.VMEM((PLANES, 4, held_rows + pieces, two), BF),
            pltpu.VMEM((first_count, 2, 4, depth, half), BF),
            pltpu.VMEM((4, 32, half), BF),
            pltpu.VMEM((PLANES, 4, 32, half), BF),
            pltpu.VMEM((PLANES, 4, rows, first_count * two), BF),
            pltpu.VMEM((wide, two + PLANES * wide), BF),
            pltpu.VMEM((PLANES, PLANES, 4 * pieces, wide), F32),
            pltpu.VMEM((2, first_count * two, two), BF),
            pltpu.VMEM((PLANES, 4 * rows, wide), F32),
            pltpu.VMEM((4 * wide, PLANES * wide), BF),
            pltpu.VMEM((PLANES, 4, 32, wide), BF),
            pltpu.VMEM((4, PLANES, 32, wide), BF),
            dma((8,)), dma((4, PLANES)), dma((PLANES, 4)), dma((3, first_count)), dma((4, first_count)),
            dma((2, PLANES, 4)), dma((PLANES, 2)), dma((4, PLANES)), dma((4, PLANES)),
        ],
        compiler_params=pltpu.CompilerParams(
            collective_id=0, has_side_effects=True, vmem_limit_bytes=40 * 2 ** 20
        ),
    )(*[pltpu.with_memory_space_constraint(v, pltpu.HBM) for v in (
        prefix.reshape(held_rows, twice_width), pair_prefix.T, pair_suffix.T, merge_count[None],
        routes, first_suffix, suffix[0], cap.transpose(0, 2, 1),
    )])
    return out.reshape(pieces, rows_piece, wide)


def on_device(prefix, first_suffix, pair_prefix, pair_suffix, merge_count, suffix, routes, cap):
    pieces = pair_prefix.shape[0]
    listed = routes.shape[1]
    owners = lax.axis_size("bits")
    slots = min(pieces, max(2, (2 * pieces * listed + owners - 1) // owners))
    held, rows_piece, twice_width = prefix.shape
    wide = 2 * cap.shape[2]
    fits = (
        owners == 4 * PLANES and wide == 128 and pieces == 8 and rows_piece == 16
        and twice_width == 2 * PLANES * wide and first_suffix.shape[0] * held == rows_piece
        and held * rows_piece * first_suffix.shape[0] == 2 * wide and suffix.shape[0] == 1
        and owners * first_suffix.shape[2] == twice_width // 2 and owners <= wide - rows_piece
    )
    body = on_device_sparse
    if slots == pieces:
        body = on_device_planes if fits else on_device_dense
    return body(
        prefix, first_suffix, pair_prefix, pair_suffix, merge_count, suffix, routes, cap
    )


def solution(mesh):
    return jax.shard_map(
        on_device,
        mesh=mesh,
        in_specs=(
            P(("grp", "bits"), None, None),
            P("grp", None, "bits", None),
            P(("grp", "bits"), None),
            P(("grp", "bits"), None),
            P(("grp", "bits")),
            P(("grp", "bits"), None, None, None),
            P(("grp", "bits"), None),
            P(),
        ),
        out_specs=P(("grp", "bits"), None, None),
        check_vma=False,
    )
```

```python
import jax
import jax.numpy as jnp
from jax import lax
from jax.experimental import pallas as pl
from jax.experimental.pallas import tpu as pltpu
from jax.sharding import PartitionSpec as P

HIGHEST_PRECISION = lax.Precision.HIGHEST


def complex_form(blocks):
    real_part = blocks[..., 0, :, :]
    imag_part = blocks[..., 1, :, :]
    upper_half = jnp.concatenate([real_part, imag_part], axis=-1)
    lower_half = jnp.concatenate([-imag_part, real_part], axis=-1)
    return jnp.concatenate([upper_half, lower_half], axis=-2)


def on_device_sparse(prefix, first_suffix, pair_prefix, pair_suffix, merge_count, suffix, routes, cap):
    pieces = pair_prefix.shape[0]
    merges = pair_prefix.shape[1]
    held_blocks = prefix.shape[0]
    rows_piece = prefix.shape[1]
    twice_width = prefix.shape[2]
    half_width = twice_width // 2
    first_count = first_suffix.shape[0]
    listed = routes.shape[1]
    owners = lax.axis_size("bits")
    slot_count = min(pieces, max(2, (2 * pieces * listed + owners - 1) // owners))
    live_mask = lax.broadcasted_iota(jnp.int32, (pieces, merges), 1) < merge_count[:, None]
    matches = (
        pair_suffix[:, :, None] == lax.broadcasted_iota(jnp.int32, (pieces, merges, first_count), 2)
    ) & live_mask[:, :, None]
    which_block = pair_prefix[:, :, None] == lax.broadcasted_iota(
        jnp.int32, (pieces, merges, held_blocks), 2
    )
    prefix_picks = jnp.einsum(
        "ika,ikp->iap", matches.astype(jnp.float32), which_block.astype(jnp.float32)
    ).astype(jnp.bfloat16)
    selected = jnp.einsum(
        "iap,prc->airc", prefix_picks, prefix, preferred_element_type=jnp.float32
    ).astype(jnp.bfloat16)
    selected = selected.reshape(first_count, pieces * rows_piece, twice_width)
    portion = lax.all_gather(first_suffix, "bits", axis=2, tiled=True)
    count_rows = portion.shape[2]
    real_cols = lax.slice_in_dim(selected, 0, count_rows, axis=2)
    imag_cols = lax.dynamic_slice_in_dim(selected, half_width, count_rows, 2)
    left_side = jnp.concatenate([real_cols, imag_cols], axis=2)
    upper_half = jnp.concatenate([portion[:, 0], portion[:, 1]], axis=2)
    lower_half = jnp.concatenate([-portion[:, 1], portion[:, 0]], axis=2)
    right_side = jnp.concatenate([upper_half, lower_half], axis=1)
    state_rows = jnp.einsum(
        "arc,acw->rw", left_side, right_side, preferred_element_type=jnp.float32
    )
    state_rows = state_rows.astype(jnp.bfloat16).reshape(pieces, rows_piece, twice_width)
    named_by = jnp.sum(
        (routes[:, :, None] == lax.broadcasted_iota(jnp.int32, (pieces, listed, owners), 2)).astype(
            jnp.int32
        ),
        axis=1,
    )
    earlier = lax.broadcasted_iota(jnp.int32, (pieces, pieces), 0) > lax.broadcasted_iota(
        jnp.int32, (pieces, pieces), 1
    )
    slot_rank = jnp.einsum(
        "ij,jd->id", earlier.astype(jnp.float32), named_by.astype(jnp.float32),
        precision=HIGHEST_PRECISION,
    ).astype(jnp.int32)
    slot_hit = (
        slot_rank[:, :, None] == lax.broadcasted_iota(jnp.int32, (pieces, owners, slot_count), 2)
    ) & (named_by[:, :, None] > 0)
    dispatch = jnp.transpose(slot_hit, (1, 2, 0)).astype(jnp.bfloat16)
    outgoing = jnp.einsum(
        "dmi,irc->dmrc", dispatch, state_rows, preferred_element_type=jnp.float32
    ).astype(jnp.bfloat16)
    own_form = complex_form(suffix[0])
    cap_form = complex_form(cap)
    products = jnp.einsum(
        "smrc,cw->smrw",
        lax.all_to_all(outgoing, "bits", split_axis=0, concat_axis=0, tiled=True),
        own_form,
        preferred_element_type=jnp.float32,
    ).astype(jnp.bfloat16)
    capped_terms = jnp.einsum(
        "smrw,wv->smrv", products, cap_form, preferred_element_type=jnp.float32
    )
    returned = lax.all_to_all(
        capped_terms.astype(jnp.bfloat16), "bits", split_axis=0, concat_axis=0, tiled=True
    ).astype(capped_terms.dtype)
    return jnp.einsum(
        "dmi,dmrv->irv", dispatch.astype(jnp.float32), returned, precision=HIGHEST_PRECISION
    )


def weights_of(pair_prefix, pair_suffix, merge_count, held_blocks, first_count):
    pieces, merges = pair_prefix.shape
    live_mask = lax.broadcasted_iota(jnp.int32, (pieces, merges), 1) < merge_count[:, None]
    matches = (
        pair_suffix[:, :, None] == lax.broadcasted_iota(jnp.int32, (pieces, merges, first_count), 2)
    ) & live_mask[:, :, None]
    which_block = pair_prefix[:, :, None] == lax.broadcasted_iota(
        jnp.int32, (pieces, merges, held_blocks), 2
    )
    return jnp.sum(
        (matches[:, :, :, None] & which_block[:, :, None, :]).astype(jnp.float32), axis=1
    ).astype(jnp.bfloat16)


def on_device_dense(prefix, first_suffix, pair_prefix, pair_suffix, merge_count, suffix, routes, cap):
    pieces = pair_prefix.shape[0]
    held_blocks, rows_piece, twice_width = prefix.shape
    first_count = first_suffix.shape[0]
    owners = lax.axis_size("bits")
    listed = routes.shape[1]
    portion = lax.all_gather(first_suffix, "bits", axis=2, tiled=True)
    cap_form = jnp.concatenate([cap[0], cap[1]], axis=1)
    cap_turn = jnp.concatenate([-cap[1], cap[0]], axis=1)
    closed = (
        jnp.dot(suffix[0, 0], cap_form, preferred_element_type=jnp.float32)
        + jnp.dot(suffix[0, 1], cap_turn, preferred_element_type=jnp.float32)
    ).astype(jnp.bfloat16)
    closed_all = lax.all_gather(closed, "bits", axis=1, tiled=False)
    picks = weights_of(pair_prefix, pair_suffix, merge_count, held_blocks, first_count)
    selected = jnp.einsum(
        "iap,prc->airc", picks, prefix, preferred_element_type=jnp.float32
    ).astype(jnp.bfloat16)
    selected = selected.reshape(first_count, pieces * rows_piece, twice_width)
    half = twice_width // 2
    real = selected[:, :, :half]
    imag = selected[:, :, half:]
    by_real = jnp.einsum(
        "arc,acw->rw", jnp.concatenate([real, -imag], axis=2),
        portion.reshape(first_count, twice_width, half), preferred_element_type=jnp.float32,
    )
    by_imag = jnp.einsum(
        "arc,acw->rw", jnp.concatenate([imag, real], axis=2),
        portion.reshape(first_count, twice_width, half), preferred_element_type=jnp.float32,
    )
    state_real = by_real.astype(jnp.bfloat16)
    state_imag = by_imag.astype(jnp.bfloat16)
    flat = closed_all.reshape(half, -1)
    capw = cap.shape[2]
    stacked = jnp.concatenate([state_real, state_imag], axis=0)
    both = jnp.dot(stacked, flat, preferred_element_type=jnp.float32)
    both = both.reshape(2, pieces, rows_piece, owners, 2, capw)
    named = jnp.sum(
        (routes[:, :, None] == lax.broadcasted_iota(jnp.int32, (pieces, listed, owners), 2)).astype(
            jnp.float32
        ),
        axis=1,
    )
    summed = jnp.sum(both * named[None, :, None, :, None, None], axis=3)
    out_real = summed[0, :, :, 0] - summed[1, :, :, 1]
    out_imag = summed[0, :, :, 1] + summed[1, :, :, 0]
    return jnp.concatenate([out_real, out_imag], axis=-1)


BF = jnp.bfloat16
F32 = jnp.float32


def flip(value, pattern):
    bit = 1
    while bit <= pattern:
        if pattern & bit:
            value = value + bit - 2 * bit * ((value // bit) % 2)
        bit *= 2
    return value


def iota(shape, axis):
    return lax.broadcasted_iota(jnp.int32, shape, axis)


PLANES = 4


def both_parts(real, imag, lanes):
    count = real.shape[0] // 16
    stacked = jnp.stack(
        [real.reshape(count, 16, lanes), imag.reshape(count, 16, lanes)], axis=1
    )
    return stacked.reshape(2 * real.shape[0], lanes)


def planes_kernel(
    sizes, x_hbm, pp_hbm, ps_hbm, count_hbm, route_hbm, f_hbm, s_hbm, cap_hbm, out_ref,
    x_ref, pp_ref, ps_ref, count_ref, route_ref, cap_ref, s_ref, qsend, qall, fall, mt, mall, sel, xy, masks, gall, acc, place, ret_out, ret_in,
    local, q_send, q_recv, f_send, f_recv, m_send, m_recv, r_send, r_recv,
):
    first_count, held, rows_piece, pieces, depth, half, wide = sizes
    rows = pieces * rows_piece
    held_rows = held * rows_piece
    span = half // PLANES
    base = first_count * held
    two = 2 * wide
    me = lax.axis_index("bits")
    z = me // 4
    j = me % 4
    y = j // 2
    middle = (z == 1) | (z == 2)

    def near(pattern):
        return flip(z, pattern)

    def beside(pattern):
        return flip(j, pattern)

    def send(src, dst, send_sem, recv_sem, plane, seat):
        return pltpu.make_async_remote_copy(
            src_ref=src, dst_ref=dst, send_sem=send_sem, recv_sem=recv_sem,
            device_id={"bits": 4 * plane + seat}, device_id_type=pl.DeviceIdType.MESH,
        )

    barrier = pltpu.get_barrier_semaphore()
    for p in (1, 2, 3, 0):
        for s in range(4):
            if p or s:
                pl.semaphore_signal(
                    barrier, inc=1, device_id={"bits": 4 * near(p) + beside(s)},
                    device_id_type=pl.DeviceIdType.MESH,
                )
    pairs = (
        (x_hbm, x_ref), (pp_hbm, pp_ref), (ps_hbm, ps_ref), (count_hbm, count_ref),
        (route_hbm, route_ref), (cap_hbm, cap_ref), (s_hbm, s_ref), (f_hbm, fall.at[:, :, j]),
    )
    loads = [pltpu.make_async_copy(a, b, local.at[i]) for i, (a, b) in enumerate(pairs)]
    for i in (6, 5, 0, 1, 2, 3, 4, 7):
        loads[i].start()

    line = iota((wide, two), 0)
    xy[:, :two] = jnp.where(iota((wide, two), 1) // rows_piece == line, 1.0, 0.0).astype(BF)
    reach = PLANES * wide
    line = iota((wide, reach), 0)
    xy[:, two:] = jnp.where(iota((wide, reach), 1) // 32 + base == line, 1.0, 0.0).astype(BF)
    for q in range(4):
        lane = iota((wide, reach), 0)
        col = iota((wide, reach), 1)
        inside = lane % 32
        goal = (lane // 32) * wide + (inside // 16) * (wide // 2) + 16 * q + inside % 16
        place[q * wide:(q + 1) * wide, :] = jnp.where(col == goal, 1.0, 0.0).astype(BF)

    for i in (1, 2, 3, 4, 0):
        loads[i].wait()
    eye = iota((pieces, pieces), 0) == iota((pieces, pieces), 1)

    def column(row):
        spread = jnp.broadcast_to(row, (pieces, pieces))
        return jnp.sum(jnp.where(eye, spread, 0), axis=1, keepdims=True)

    spot = iota((pieces, wide), 1)
    count = column(count_ref[...])
    table = jnp.zeros((pieces, wide), F32)
    for k in range(pp_ref.shape[0]):
        code = column(ps_ref[k:k + 1, :]) * held + column(pp_ref[k:k + 1, :])
        table = table + jnp.where((spot == code) & (count > k), 1.0, 0.0)
    for k in range(route_ref.shape[1]):
        table = table + jnp.where(spot == route_ref[:, k:k + 1] + base, 1.0, 0.0)
    table = table.astype(BF)
    for p in range(PLANES):
        qsend[p, :held_rows, :wide] = x_ref[:, p * span:(p + 1) * span]
        qsend[p, :held_rows, wide:] = x_ref[:, half + p * span:half + (p + 1) * span]
        qsend[p, held_rows:, :wide] = table
        qsend[p, held_rows:, wide:] = jnp.zeros((pieces, wide), BF)
    qall[z, j] = qsend[z]

    loads[5].wait()
    loads[6].wait()

    def times(left, part):
        return lax.dot_general(
            left, s_ref[part], (((1,), (1,)), ((), ())), preferred_element_type=F32
        )

    upper = both_parts(cap_ref[0], cap_ref[1], half)
    lower = both_parts(-cap_ref[1], cap_ref[0], half)
    closed = (times(upper, 0) + times(lower, 1)).astype(BF)
    mt[...] = closed.reshape(4, 32, half)
    mall[z, j] = mt[j]

    def m_near(t, s):
        return send(
            mt.at[beside(s)], mall.at[z, j], m_send.at[0, t, s], m_recv.at[z, y], near(t),
            beside(s),
        )

    def m_quad(s):
        side = flip(y, 1) if False else y
        return send(
            mt.at[beside(s)], mall.at[z, j], m_send.at[0, 0, s], m_recv.at[z, side], z, beside(s)
        )

    def m_pair(source, side, t, index):
        block = mall.at[source, pl.ds(2 * side, 2)]
        return send(
            block, block, m_send.at[1, t, index], m_recv.at[source, side], near(t), j
        )

    def m_arrived(source, side):
        block = mall.at[source, pl.ds(2 * side, 2)]
        send(block, block, m_send.at[0, 0, 0], m_recv.at[source, side], z, beside(1)).wait_recv()

    def q_line(t):
        return send(
            qsend.at[near(t)], qall.at[z, j], q_send.at[0, t], q_recv.at[z, j], near(t), j
        )

    def q_pass(t, s, to):
        block = qall.at[near(t), beside(s)]
        return send(
            block, block, q_send.at[to + s // 2, t], q_recv.at[near(t), beside(s)], z, beside(to)
        )

    def q_arrived(t, s):
        block = qall.at[near(t), beside(s)]
        send(
            block, block, q_send.at[0, 0], q_recv.at[near(t), beside(s)], z, beside(1)
        ).wait_recv()

    cuts = [(0, first_count // 2)] + [(a, 1) for a in range(first_count // 2, first_count)]

    def f_block(i, seat):
        first, size = cuts[i]
        return fall.at[pl.ds(first, size), :, seat]

    def f_copy(s, i):
        first, size = cuts[i]
        return send(
            f_hbm.at[pl.ds(first, size)], f_block(i, j), f_send.at[s, i], f_recv.at[j, i], z,
            beside(s),
        )

    def f_pass(i):
        block = f_block(i, beside(2))
        return send(block, block, f_send.at[0, i], f_recv.at[beside(2), i], z, beside(1))

    def f_arrived(s, i):
        block = f_block(i, beside(s))
        send(block, block, f_send.at[0, i], f_recv.at[beside(s), i], z, beside(1)).wait_recv()

    same = jnp.where(
        iota((rows_piece, two), 0) == iota((rows_piece, two), 1) % rows_piece, 1.0, 0.0
    ).astype(F32)

    group_of = [
        jnp.where(iota((rows, two), 1) // held_rows == a, 1.0, 0.0).astype(BF)
        for a in range(first_count)
    ]

    def prepare(t):
        plane = near(t)
        tabs = jnp.concatenate(
            [qall[plane, q, held_rows:, :wide].astype(F32) for q in range(4)], axis=0
        ).astype(BF)
        spread = jnp.dot(tabs, xy[...], preferred_element_type=F32)
        for p in range(PLANES):
            masks[p, plane] = spread[:, two + p * wide:two + (p + 1) * wide]
        for q in range(4):
            wanted = spread[q * pieces:(q + 1) * pieces, :two]
            kept = jnp.broadcast_to(wanted[:, None, :], (pieces, rows_piece, two)) * same[None]
            kept = kept.reshape(rows, two).astype(BF)
            left = jnp.concatenate([kept * group_of[a] for a in range(first_count)], axis=0)
            right = jnp.concatenate([qall[plane, q, :held_rows]] * first_count, axis=0)
            picked = jnp.dot(left, right, preferred_element_type=F32).astype(BF)
            for a in range(first_count):
                sel[plane, q, :, a * two:(a + 1) * two] = picked[a * rows:(a + 1) * rows]

    def gather(b, planes):
        caps = jnp.concatenate([mall[p].reshape(wide, half) for p in planes], axis=0)
        split = caps.reshape(4 * len(planes), 2, 16, half)
        turned = jnp.stack([-split[:, 1], split[:, 0]], axis=1).reshape(caps.shape)
        right = jnp.concatenate(
            [jnp.concatenate([caps, turned], axis=1), jnp.concatenate([turned, -caps], axis=1)],
            axis=0,
        )
        left = jnp.concatenate(
            [fall[:, r].reshape(first_count * wide, half) for r in range(2)], axis=1
        )
        product = lax.dot_general(
            left, right, (((1,), (1,)), ((), ())), preferred_element_type=F32
        ).astype(BF)
        for a in range(first_count):
            for r in range(2):
                gall[b, a * two + r * wide:a * two + (r + 1) * wide] = product[
                    a * wide:(a + 1) * wide, r * two:(r + 1) * two
                ]

    def part(b, planes, owner):
        lines = sel[owner].reshape(4 * rows, first_count * two)
        values = jnp.dot(lines, gall[b], preferred_element_type=F32)
        total = None
        for u, p in enumerate(planes):
            mask = masks[p, owner].reshape(4 * pieces, 1, wide)
            mask = jnp.broadcast_to(mask, (4 * pieces, rows_piece, wide))
            term = values[:, u * wide:(u + 1) * wide] * mask.reshape(4 * rows, wide)
            total = term if total is None else total + term
        return total

    pl.semaphore_wait(barrier, 4 * PLANES - 1)
    far = flip(y, 1)
    early = (z, near(1))

    def q_spread(t):
        q_arrived(t, 0)
        for to in (2, 1):
            q_pass(t, 0, to).start()

    def q_second(t):
        q_arrived(t, 2)
        q_pass(t, 2, 1).start()

    def q_rest(t):
        q_arrived(t, 1)
        q_arrived(t, 3)

    edge = jnp.logical_not(middle)
    for s in (2, 3):
        m_quad(s).start()
    for t in (3, 2, 1):
        q_line(t).start()
    for to in (2, 1):
        q_pass(0, 0, to).start()
    m_quad(1).start()
    q_arrived(0, 1)

    @pl.when(edge)
    def _():
        for s in (0, 1):
            m_near(2, s).start()

    @pl.when(middle)
    def _():
        for s in (0, 1):
            m_near(1, s).start()

    f_copy(2, 0).start()
    for i in range(len(cuts)):
        f_copy(1, i).start()
    m_arrived(z, far)

    @pl.when(middle)
    def _():
        for t in (1, 3):
            m_pair(z, far, t, 0).start()

    @pl.when(edge)
    def _():
        m_pair(z, far, 2, 0).start()
        for s in (0, 1):
            m_near(1, s).start()
        m_pair(z, far, 1, 0).start()

    f_copy(2, 1).start()
    q_second(0)
    q_spread(1)

    @pl.when(middle)
    def _():
        for t in (2, 3):
            for s in (0, 1):
                m_near(t, s).start()

    q_arrived(0, 3)
    prepare(0)
    q_spread(2)
    q_spread(3)
    for i in range(2, len(cuts)):
        f_copy(2, i).start()

    @pl.when(middle)
    def _():
        m_arrived(near(2), y)
        m_pair(near(2), y, 1, 1).start()

    q_second(1)

    @pl.when(middle)
    def _():
        m_arrived(near(2), far)
        m_pair(near(2), far, 1, 3).start()
        m_arrived(near(3), far)
        m_pair(near(3), far, 1, 2).start()

    f_arrived(2, 0)
    f_pass(0).start()
    q_second(2)
    q_second(3)

    f_arrived(2, 1)
    f_pass(1).start()
    q_rest(1)
    prepare(1)
    q_rest(2)
    prepare(2)
    for i in range(2, len(cuts)):
        f_arrived(2, i)
        f_pass(i).start()
    q_rest(3)
    prepare(3)
    send(
        mt.at[j], mall.at[z, beside(1)], m_send.at[0, 0, 0], m_recv.at[z, y], z, beside(1)
    ).wait_recv()
    loads[7].wait()
    m_arrived(near(1), y)
    m_arrived(near(1), far)
    for s in (1, 3):
        for i in range(len(cuts)):
            f_arrived(s, i)
    gather(0, early)
    for t in (3, 2):
        acc[near(t)] = part(0, early, near(t))

    @pl.when(jnp.logical_not(middle))
    def _():
        m_arrived(near(2), y)
        m_arrived(near(2), far)
        m_arrived(near(3), far)

    m_arrived(near(3), y)
    late = (near(2), near(3))
    gather(1, late)

    def ret_copy(t, s):
        return send(
            ret_out.at[near(t), beside(s)], ret_in.at[j, z], r_send.at[s, t], r_recv.at[j, z],
            near(t), beside(s),
        )

    group = iota((32, wide), 1) // 32
    for ends in ((3, 2), (1, 0)):
        for t in ends:
            owner = near(t)
            total = acc[owner] if t > 1 else part(0, early, owner)
            total = (total + part(1, late, owner)).reshape(4, 4, 32, wide)
            packed = None
            for k in range(4):
                mixed = total[:, (3 - k) % 4]
                for m in (2, 1, 0):
                    mixed = jnp.where(group == m, total[:, (m - k) % 4], mixed)
                if k:
                    mixed = pltpu.roll(mixed, wide - 32 * k, 2)
                packed = mixed if packed is None else packed + mixed
            ret_out[owner] = packed.astype(BF)
        for t in ends:
            for s in (3, 2, 1, 0):
                if s or t:
                    ret_copy(t, s).start()
    ret_in[j, z] = ret_out[z, j]
    for t in range(PLANES):
        for s in (0, 1, 2, 3):
            if s or t:
                block = ret_in.at[beside(s), near(t)]
                send(
                    block, block, r_send.at[0, 0], r_recv.at[beside(s), near(t)], z, beside(1)
                ).wait_recv()
    left = jnp.concatenate([ret_in[q].reshape(wide, wide) for q in range(4)], axis=1)
    placed = jnp.dot(left, place[...], preferred_element_type=F32).reshape(PLANES, 32, reach)
    summed = jnp.sum(placed, axis=0)
    for b in range(4):
        out_ref[b * 32:(b + 1) * 32] = summed[:, b * wide:(b + 1) * wide]

    for s in (2, 3, 1):
        m_quad(s).wait_send()
    for s in (0, 1):
        for t in (2, 1):
            m_near(t, s).wait_send()
    m_pair(z, far, 1, 0).wait_send()

    @pl.when(middle)
    def _():
        for s in (0, 1):
            m_near(3, s).wait_send()
        m_pair(z, far, 3, 0).wait_send()
        m_pair(near(2), y, 1, 1).wait_send()
        m_pair(near(3), far, 1, 2).wait_send()
        m_pair(near(2), far, 1, 3).wait_send()

    @pl.when(jnp.logical_not(middle))
    def _():
        m_pair(z, far, 2, 0).wait_send()

    for t in (3, 2, 1):
        q_line(t).wait_send()
    for t in range(PLANES):
        for to in (2, 1):
            q_pass(t, 0, to).wait_send()
        q_pass(t, 2, 1).wait_send()
    for i in range(len(cuts)):
        for s in (2, 1):
            f_copy(s, i).wait_send()
        f_pass(i).wait_send()
    for s in range(4):
        for t in range(PLANES):
            if s or t:
                ret_copy(t, s).wait_send()


def on_device_planes(prefix, first_suffix, pair_prefix, pair_suffix, merge_count, suffix, routes, cap):
    pieces = pair_prefix.shape[0]
    held, rows_piece, twice_width = prefix.shape
    half = twice_width // 2
    first_count, _, depth, _ = first_suffix.shape
    wide = 2 * cap.shape[2]
    rows = pieces * rows_piece
    held_rows = held * rows_piece
    two = 2 * wide
    sizes = (first_count, held, rows_piece, pieces, depth, half, wide)
    vmem = pl.BlockSpec(memory_space=pltpu.VMEM)
    hbm = pl.BlockSpec(memory_space=pltpu.HBM)
    dma = pltpu.SemaphoreType.DMA
    out = pl.pallas_call(
        lambda *refs: planes_kernel(sizes, *refs),
        name="planes",
        out_shape=jax.ShapeDtypeStruct((rows, wide), F32),
        in_specs=[hbm] * 8,
        out_specs=vmem,
        scratch_shapes=[
            pltpu.VMEM((held_rows, twice_width), BF),
            pltpu.VMEM(pair_prefix.shape[::-1], jnp.int32),
            pltpu.VMEM(pair_prefix.shape[::-1], jnp.int32),
            pltpu.VMEM((1, pieces), jnp.int32),
            pltpu.VMEM(routes.shape, jnp.int32),
            pltpu.VMEM((2, wide // 2, half), BF),
            pltpu.VMEM((2, half, half), BF),
            pltpu.VMEM((PLANES, held_rows + pieces, two), BF),
            pltpu.VMEM((PLANES, 4, held_rows + pieces, two), BF),
            pltpu.VMEM((first_count, 2, 4, depth, half), BF),
            pltpu.VMEM((4, 32, half), BF),
            pltpu.VMEM((PLANES, 4, 32, half), BF),
            pltpu.VMEM((PLANES, 4, rows, first_count * two), BF),
            pltpu.VMEM((wide, two + PLANES * wide), BF),
            pltpu.VMEM((PLANES, PLANES, 4 * pieces, wide), F32),
            pltpu.VMEM((2, first_count * two, two), BF),
            pltpu.VMEM((PLANES, 4 * rows, wide), F32),
            pltpu.VMEM((4 * wide, PLANES * wide), BF),
            pltpu.VMEM((PLANES, 4, 32, wide), BF),
            pltpu.VMEM((4, PLANES, 32, wide), BF),
            dma((8,)), dma((4, PLANES)), dma((PLANES, 4)), dma((3, first_count)), dma((4, first_count)),
            dma((2, PLANES, 4)), dma((PLANES, 2)), dma((4, PLANES)), dma((4, PLANES)),
        ],
        compiler_params=pltpu.CompilerParams(
            collective_id=0, has_side_effects=True, vmem_limit_bytes=40 * 2 ** 20
        ),
    )(*[pltpu.with_memory_space_constraint(v, pltpu.HBM) for v in (
        prefix.reshape(held_rows, twice_width), pair_prefix.T, pair_suffix.T, merge_count[None],
        routes, first_suffix, suffix[0], cap.transpose(0, 2, 1),
    )])
    return out.reshape(pieces, rows_piece, wide)


def on_device(prefix, first_suffix, pair_prefix, pair_suffix, merge_count, suffix, routes, cap):
    pieces = pair_prefix.shape[0]
    listed = routes.shape[1]
    owners = lax.axis_size("bits")
    slots = min(pieces, max(2, (2 * pieces * listed + owners - 1) // owners))
    held, rows_piece, twice_width = prefix.shape
    wide = 2 * cap.shape[2]
    fits = (
        owners == 4 * PLANES and wide == 128 and pieces == 8 and rows_piece == 16
        and twice_width == 2 * PLANES * wide and first_suffix.shape[0] * held == rows_piece
        and held * rows_piece * first_suffix.shape[0] == 2 * wide and suffix.shape[0] == 1
        and owners * first_suffix.shape[2] == twice_width // 2 and owners <= wide - rows_piece
    )
    body = on_device_sparse
    if slots == pieces:
        body = on_device_planes if fits else on_device_dense
    return body(
        prefix, first_suffix, pair_prefix, pair_suffix, merge_count, suffix, routes, cap
    )


def solution(mesh):
    return jax.shard_map(
        on_device,
        mesh=mesh,
        in_specs=(
            P(("grp", "bits"), None, None),
            P("grp", None, "bits", None),
            P(("grp", "bits"), None),
            P(("grp", "bits"), None),
            P(("grp", "bits")),
            P(("grp", "bits"), None, None, None),
            P(("grp", "bits"), None),
            P(),
        ),
        out_specs=P(("grp", "bits"), None, None),
        check_vma=False,
    )
```
